512 devices in a mesh: gx: 32 (over z, y_lo), row: 8 (over x, core), th: 2 (over y_hi).
Axes of the slice: x: 4, y: 4 (y_hi: 2, y_lo: 2; y = y_hi * 2 + y_lo), z: 16, core: 2. Of those that a mesh axis runs over, the one named last changes fastest.
Arguments:
- state: float32 [5, 1024, 128, 256], P(None, 'gx', 'row', 'th'), may hold values from -2 to 4, as said below
- adjoint_seed: float32 [5, 1024, 128, 256], P(None, 'gx', 'row', 'th'), may hold values from -6 to 6
- coef_x: float32 [9], replicated, may hold values from -1.75 to 1.75
- coef_r: float32 [9], replicated, may hold values from -1.75 to 1.75
- coef_t: float32 [9], replicated, may hold values from -1.75 to 1.75
- coef_filter: float32 [9], replicated, may hold values from -0.625 to 0.625
- metric: float32 [128], P('row'), may hold values from 0.5 to 2
Outputs:
- new_state: float32 [5, 1024, 128, 256], P(None, 'gx', 'row', 'th')
- adjoint_state: float32 [5, 1024, 128, 256], P(None, 'gx', 'row', 'th')
The draws below stay inside these ranges and needn't reach their ends.
Inputs may be any that keep to these rules, and one draw needn't show every extreme that they name: `state`: component 0 (density) lies in [0.5, 1.5], components 1 to 3 (momenta) in [-2, 2], component 4 (total energy) in [2, 4].
All inputs are finite; a program needn't handle non-finite values.
Results may differ from the reference program's by a relative error of at most 0.0001.
Values sent between devices are 32-bit elements; how exact they have to be, the bound alone decides.
No kernel may reach another device: no remote copies, remote signals or barrier semaphores. Data moves between devices by JAX's collectives and lax.ppermute only.
A program may use at most 64 MiB of HBM per device.

```python
import math
import jax
import jax.numpy as jnp
from jax import lax

CX = 32
W = 4
NX = 1024
NR = 128
NT = 256


def draw_state(key, part):
    keys = jax.random.split(key, 3)
    shape = (NX, NR, NT)
    density = jax.random.uniform(keys[0], shape, jnp.float32, 0.7, 1.3)
    moment = jnp.clip(0.5 * jax.random.normal(keys[1], (3,) + shape, jnp.float32), -2.0, 2.0)
    energy = jax.random.uniform(keys[2], shape, jnp.float32, 2.5, 3.5)
    return jnp.concatenate([density[None], moment, energy[None]], axis=0)


def levels(own_key, dims, shards, least, high):
    gain = 1.0
    for axis_at, parts in shards:
        draws = jax.random.uniform(jax.random.fold_in(jax.random.fold_in(own_key, 6), axis_at), (parts,), jnp.float32, least / len(shards), high / len(shards))
        gain = gain * jnp.repeat(jnp.exp(draws), dims[axis_at] // parts).reshape((-1,) + (1,) * (len(dims) - 1 - axis_at))
    return gain


def gaussian(own_key, extent, spread, bound, shards=(), kind=jnp.bfloat16):
    values = spread * jax.random.normal(own_key, extent, jnp.float32)
    if shards:
        values = values * levels(own_key, extent, shards, -0.22, 0.18)
    return jnp.clip(values, -bound, bound).astype(kind)


def setup_inputs(seed: int = 0) -> dict:
    streams_of = jax.random.split(jax.random.key(seed), 8)
    return {
        "state": draw_state(jax.random.fold_in(streams_of[7], 71), 0),
        "adjoint_seed": gaussian(streams_of[1], (5, NX, NR, NT), 1.0, 6.0, ((1, 32), (2, 8), (3, 2)), jnp.float32),
        "coef_x": gaussian(streams_of[2], (2 * W + 1,), 0.3, 1.75, (), jnp.float32),
        "coef_r": gaussian(streams_of[3], (2 * W + 1,), 0.3, 1.75, (), jnp.float32),
        "coef_t": gaussian(streams_of[4], (2 * W + 1,), 0.3, 1.75, (), jnp.float32),
        "coef_filter": gaussian(streams_of[5], (2 * W + 1,), 0.1, 0.625, (), jnp.float32),
        "metric": jnp.clip(jnp.exp(math.log(2.0) - 1.3862944 * jax.random.uniform(streams_of[6], (NR,), jnp.float32) ** levels(streams_of[6], (NR,), ((0, 8),), -0.2, 0.2)), 0.5, 2.0),
    }


section_dt = 0.1
gamma_less = 0.4

def fluxes(state):
    density = state[0]
    velocity = state[1:4] / density
    pressure = gamma_less * (state[4] - 0.5 * lax.optimization_barrier(jnp.sum(state[1:4] * velocity, axis=0)))
    enthalpy = state[4] + pressure
    result = []
    for direction in range(3):
        speed = velocity[direction]
        moment = state[1:4] * speed
        moment = moment.at[direction].add(pressure)
        result.append(jnp.concatenate([state[1 + direction][None], moment, (enthalpy * speed)[None]], axis=0))
    return result

def stencil_sum(field, coef, axis, periodic):
    reach = (coef.shape[0] - 1) // 2
    widths = [(0, 0)] * field.ndim
    widths[axis] = (reach, reach)
    if periodic:
        padded = jnp.pad(field, widths, mode='wrap')
    else:
        padded = jnp.pad(field, widths)
    count = field.shape[axis]
    total = jnp.zeros(field.shape, field.dtype)
    for tap in range(coef.shape[0]):
        total = total + coef[tap] * lax.slice_in_dim(padded, tap, tap + count, axis=axis)
    return total

def slab_sum(field, coef, low, count):
    reach = (coef.shape[0] - 1) // 2
    shape = (field.shape[0], count, field.shape[2], field.shape[3])
    total = jnp.zeros(shape, field.dtype)
    for tap in range(coef.shape[0]):
        begin = low + tap - reach
        total = total + coef[tap] * lax.slice_in_dim(field, begin, begin + count, axis=1)
    return total

def reference(state, adjoint_seed, coef_x, coef_r, coef_t, coef_filter, metric):
    margin = 2 * W
    width = CX + 4 * W
    total_x = state.shape[1]
    filler = jnp.array([1.0, 0.0, 0.0, 0.0, 3.0], dtype=state.dtype)[:, None, None, None]
    padded_state = jnp.pad(state - filler, ((0, 0), (margin, margin), (0, 0), (0, 0))) + filler
    padded_adjoint = jnp.pad(adjoint_seed, ((0, 0), (margin, margin), (0, 0), (0, 0)))
    weight_r = metric[None, None, :, None]
    flip_filter = coef_filter[::-1]
    flip_x = coef_x[::-1]
    flip_r = coef_r[::-1]
    flip_t = coef_t[::-1]

    def block(index, outs):
        new_out, adj_out = outs
        start = (index * CX).astype(jnp.int32)
        slab = lax.dynamic_slice_in_dim(padded_state, start, width, axis=1)
        seed_slab = lax.dynamic_slice_in_dim(padded_adjoint, start, width, axis=1)
        position = start - margin + jnp.arange(width, dtype=jnp.int32)
        inside = ((position >= 0) & (position < total_x))[None, :, None, None]
        flux_x, flux_r, flux_t = fluxes(slab)
        flux_x = jnp.where(inside, flux_x, 0.0)
        span = CX + 2 * W
        mid_inside = inside[:, W:W + span]
        resid = -(slab_sum(flux_x, coef_x, W, span) + stencil_sum(flux_r[:, W:W + span], coef_r, 2, False) + weight_r * stencil_sum(flux_t[:, W:W + span], coef_t, 3, True))
        section = slab[:, W:W + span] + section_dt * resid
        section = jnp.where(mid_inside, section, 0.0)
        new_block = section[:, W:W + CX] - slab_sum(section, coef_filter, W, CX)
        lam_section = seed_slab[:, W:W + span] - slab_sum(seed_slab, flip_filter, W, span)
        lam_section = jnp.where(mid_inside, lam_section, 0.0)
        lam_resid = section_dt * lam_section
        grad_x = -slab_sum(lam_resid, flip_x, W, CX)
        lam_inner = lam_resid[:, W:W + CX]
        grad_r = -stencil_sum(lam_inner, flip_r, 2, False)
        grad_t = -stencil_sum(weight_r * lam_inner, flip_t, 3, True)
        _, pull = jax.vjp(fluxes, slab[:, margin:margin + CX])
        flux_grad, = pull([grad_x, grad_r, grad_t])
        adj_block = lam_section[:, W:W + CX] + flux_grad
        zero = jnp.zeros((), jnp.int32)
        new_out = lax.dynamic_update_slice(new_out, new_block, (zero, start, zero, zero))
        adj_out = lax.dynamic_update_slice(adj_out, adj_block, (zero, start, zero, zero))
        return (new_out, adj_out)
    empty = jnp.zeros(state.shape, state.dtype)
    new_state, adjoint_state = lax.fori_loop(0, total_x // CX, block, (empty, empty))
    return (new_state, adjoint_state)
```

```python
import functools

import jax
import jax.numpy as jnp
from jax import lax
from jax.experimental import pallas as pl
from jax.experimental.pallas import tpu as pltpu
from jax.sharding import PartitionSpec as P

DT = 0.1
GAM = 0.4
W = 4
TAPS = 9
C = 5
NX, NR, NT = 32, 16, 128
F32 = jnp.float32
BF16 = jnp.bfloat16
VM = pl.BlockSpec(memory_space=pltpu.VMEM)
SM = pl.BlockSpec(memory_space=pltpu.SMEM)
ANY = pl.BlockSpec(memory_space=pl.ANY)


def prims(q):
    inv = 1.0 / q[0]
    u, v, w = q[1] * inv, q[2] * inv, q[3] * inv
    p = GAM * (q[4] - 0.5 * (q[1] * u + q[2] * v + q[3] * w))
    return inv, u, v, w, p, q[4] + p


def flux_x(q, pr):
    _, u, _, _, p, h = pr
    return [q[1], q[1] * u + p, q[2] * u, q[3] * u, h * u]


def flux_r(q, pr):
    _, _, v, _, p, h = pr
    return [q[2], q[1] * v, q[2] * v + p, q[3] * v, h * v]


def flux_t(q, pr):
    _, _, _, w, p, h = pr
    return [q[3], q[1] * w, q[2] * w, q[3] * w + p, h * w]


def pull(q, pr, a, b, c):
    inv, u, v, w, _, h = pr
    ub = a[1] * q[1] + a[2] * q[2] + a[3] * q[3] + a[4] * h
    vb = b[1] * q[1] + b[2] * q[2] + b[3] * q[3] + b[4] * h
    wb = c[1] * q[1] + c[2] * q[2] + c[3] * q[3] + c[4] * h
    hb = a[4] * u + b[4] * v + c[4] * w
    pb = a[1] + b[2] + c[3] + hb
    s = (-0.5 * GAM) * pb
    ub = (ub + s * q[1]) * inv
    vb = (vb + s * q[2]) * inv
    wb = (wb + s * q[3]) * inv
    o1 = a[0] + (a[1] + s) * u + b[1] * v + c[1] * w + ub
    o2 = b[0] + a[2] * u + (b[2] + s) * v + c[2] * w + vb
    o3 = c[0] + a[3] * u + b[3] * v + (c[3] + s) * w + wb
    o4 = hb + GAM * pb
    o0 = -(ub * u + vb * v + wb * w)
    return [o0, o1, o2, o3, o4]


def pull_x(q, pr, a):
    inv, u, v, w, _, h = pr
    hb = a[4] * u
    pb = a[1] + hb
    s = (-0.5 * GAM) * pb
    ub = (a[1] * q[1] + a[2] * q[2] + a[3] * q[3] + a[4] * h + s * q[1]) * inv
    vb = s * v
    wb = s * w
    o1 = a[0] + (a[1] + s) * u + ub
    o2 = a[2] * u + s * v + vb
    o3 = a[3] * u + s * w + wb
    o4 = hb + GAM * pb
    o0 = -(ub * u + vb * v + wb * w)
    return [o0, o1, o2, o3, o4]


def iota(shape, dim):
    return lax.broadcasted_iota(jnp.int32, shape, dim)


def metric_tile(met):
    row = iota((NR, NT), 0)
    tile = jnp.zeros((NR, NT), F32)
    for r in range(NR):
        tile = jnp.where(row == r, met[r], tile)
    return tile


def is_even(par):
    return jnp.full((NR, NT), par, jnp.int32) == 0


def split(x):
    hi = x.astype(BF16)
    return hi, (x - hi.astype(F32)).astype(BF16)


def band(coef):
    offset = iota((NT, NT), 0) - iota((NT, NT), 1) + W
    mat = jnp.zeros((NT, NT), F32)
    for j in range(TAPS):
        mat = jnp.where(offset == j, coef[j], mat)
    return mat


def t_own(hi, lo, coef, out):
    bhi, blo = split(band(coef))
    both = jnp.concatenate([bhi, blo], axis=1)
    step = 8
    for g in range(NX // step):
        h = hi[pl.ds(g * step, step)].reshape(step * C * NR, NT)
        l = lo[pl.ds(g * step, step)].reshape(step * C * NR, NT)
        first = jnp.dot(h, both, preferred_element_type=F32)
        second = jnp.dot(l, bhi, preferred_element_type=F32)
        total = first[:, :NT] + first[:, NT:] + second
        out[pl.ds(g * step, step)] = total.reshape(step, C, NR, NT)


def t_pack_coefs(coef):
    lane = iota((NR, NT), 1) % 8
    masks = {}
    for j in range(W):
        masks[j] = jnp.where((lane >= 4) & (lane < 8 - j), coef[j], 0.0)
    for j in range(W + 1, TAPS):
        masks[j] = jnp.where((lane >= 8 - j) & (lane < 4), coef[j], 0.0)
    return masks


def t_halo_packed(rims, masks):
    total = None
    for j, m in masks.items():
        term = m * pltpu.roll(rims, (4 - j) % NT, 1)
        total = term if total is None else total + term
    return total


def t_unpack(packed, k):
    lane = iota((NR, NT), 1)
    moved = pltpu.roll(packed, 124 - 8 * k, 1)
    return jnp.where((lane < 4) | (lane >= 124), moved, 0.0)


def t_pack_into(ref, fields, xx, k):
    lane = iota((NR, NT), 1)
    for c in range(C):
        moved = pltpu.roll(fields[c], 8 * k + 4, 1)
        ref[c, xx] = jnp.where(lane // 8 == k, moved, ref[c, xx])


def r_pack(first, second, even):
    sub = iota((8, NT), 0)
    low = jnp.where(sub < 4, first[:8], pltpu.roll(second[:8], 4, 0))
    high = jnp.where(sub < 4, pltpu.roll(first[8:], 4, 0), second[8:])
    ev = even[:8]
    return jnp.where(ev, high, low), jnp.where(ev, low, high)


def r_coefs(coef):
    sub = iota((8, NT), 0)
    low = [jnp.where(sub < 4 - j, coef[j], 0.0) for j in range(W)]
    high = {j: jnp.where(sub >= 12 - j, coef[j], 0.0) for j in range(W + 1, TAPS)}
    return low, high


def r_halo(low, high, xx, coefs):
    lo_c, hi_c = coefs
    top = None
    for j in range(W):
        shift = (8 - (4 * xx + j)) % 8
        term = lo_c[j] * (pltpu.roll(low, shift, 0) if shift else low)
        top = term if top is None else top + term
    bottom = None
    for j in range(W + 1, TAPS):
        shift = (12 - j - 4 * xx) % 8
        term = hi_c[j] * (pltpu.roll(high, shift, 0) if shift else high)
        bottom = term if bottom is None else bottom + term
    return jnp.concatenate([top, bottom], axis=0)


def x_taps(read, x, coef):
    total = None
    for j in range(TAPS):
        at = x + j - W
        if isinstance(x, int) and not 0 <= at < NX:
            continue
        term = coef[j] * read(at)
        total = term if total is None else total + term
    return total


def x_halo(planes, i, low, coef):
    total = None
    for j in range(TAPS):
        at = i + j if low else i + j - 8
        if not 0 <= at < W:
            continue
        term = coef[j] * planes[at]
        total = term if total is None else total + term
    return total


def over_planes(body):
    for x in range(W):
        body(x)

    def step(x, carry):
        body(x)
        return carry

    lax.fori_loop(W, NX - W, step, 0)
    for x in range(NX - W, NX):
        body(x)


def loop(lo, hi, body):
    def step(k, carry):
        body(k)
        return carry

    lax.fori_loop(lo, hi, step, 0)


def rims_x(par, state, seed, xe, xo):
    even = par[0] == 0
    first = jnp.where(even, NX - W, 0)
    second = jnp.where(even, 0, NX - W)
    for start, out in ((first, xe), (second, xo)):
        for i in range(W):
            q = [state[c, start + i] for c in range(C)]
            f = flux_x(q, prims(q))
            for c in range(C):
                out[c, i] = f[c]
                out[C + c, i] = seed[c, start + i]


def rims_rt(par, state, re, ro, th):
    even = is_even(par[1])
    th[...] = jnp.zeros(th.shape, F32)

    def pair(k):
        keep = []
        for xx in range(2):
            q = [state[c, 2 * k + xx] for c in range(C)]
            pr = prims(q)
            keep.append(flux_r(q, pr))
            t_pack_into(th, flux_t(q, pr), xx, k)
        for c in range(C):
            re[c, k], ro[c, k] = r_pack(keep[0][c], keep[1][c], even)

    loop(0, NX // 2, pair)


def own(cx, cr, ct, cf, met, state, seed, psec, plam, fx, fr, hi, lo, tt):
    mt = metric_tile(met)
    zero = jnp.zeros((8, NT), F32)

    def fill(x):
        q = [state[c, x] for c in range(C)]
        pr = prims(q)
        f, g, h = flux_x(q, pr), flux_r(q, pr), flux_t(q, pr)
        for c in range(C):
            fx[c, x] = f[c]
            fr[c, x, 0:8] = zero
            fr[c, x, 8:24] = g[c]
            fr[c, x, 24:32] = zero
            hi[x, c], lo[x, c] = split(h[c])

    loop(0, NX, fill)
    t_own(hi, lo, ct, tt)
    fc = [cf[TAPS - 1 - j] for j in range(TAPS)]
    xc = [cx[j] for j in range(TAPS)]

    def plane(x):
        for c in range(C):
            acc = x_taps(lambda at: fx[c, at], x, xc) + mt * tt[x, c]
            for j in range(TAPS):
                acc += cr[j] * fr[c, x, 4 + j : 20 + j]
            psec[c, x] = state[c, x] - DT * acc
            plam[c, x] = seed[c, x] - x_taps(lambda at: seed[c, at], x, fc)

    over_planes(plane)


def join(par, cx, cr, ct, cf, met, psec, plam, xe, xo, re, ro, th, sec, lam, xe2, xo2, re2, ro2, th2):
    mt = metric_tile(met)
    evx, evr = is_even(par[0]), is_even(par[1])
    fc = [cf[TAPS - 1 - j] for j in range(TAPS)]
    xc = [cx[j] for j in range(TAPS)]
    for low in (True, False):
        base = 0 if low else NX - W
        for c in range(2 * C):
            near, far = (xo, xe) if low else (xe, xo)
            planes = [jnp.where(evx, near[c, i], far[c, i]) for i in range(W)]
            for i in range(W):
                if c < C:
                    sec[c, base + i] = psec[c, base + i] - DT * x_halo(planes, i, low, xc)
                else:
                    lam[c - C, base + i] = plam[c - C, base + i] - x_halo(planes, i, low, fc)
    th2[...] = jnp.zeros(th2.shape, F32)
    rc = r_coefs(cr)
    tc = t_pack_coefs(ct)
    packed = [[mt * t_halo_packed(th[c, xx], tc) for xx in range(2)] for c in range(C)]
    ev8 = evr[:8]

    def pair(k, s_ref, l_ref):
        lams = [[], []]
        for c in range(C):
            a, b = re[c, k], ro[c, k]
            low, high = jnp.where(ev8, b, a), jnp.where(ev8, a, b)
            for xx in range(2):
                x = 2 * k + xx
                share = r_halo(low, high, xx, rc) + t_unpack(packed[c][xx], k)
                sec[c, x] = s_ref[c, x] - DT * share
                value = l_ref[c, x]
                lam[c, x] = value
                lams[xx].append(value)
        for c in range(C):
            re2[c, k], ro2[c, k] = r_pack(lams[0][c], lams[1][c], evr)
        for xx in range(2):
            t_pack_into(th2, [mt * v for v in lams[xx]], xx, k)

    loop(0, 2, functools.partial(pair, s_ref=sec, l_ref=lam))
    loop(2, 14, functools.partial(pair, s_ref=psec, l_ref=plam))
    loop(14, 16, functools.partial(pair, s_ref=sec, l_ref=lam))
    even = par[0] == 0
    first = jnp.where(even, NX - W, 0)
    second = jnp.where(even, 0, NX - W)
    for start, out in ((first, xe2), (second, xo2)):
        for i in range(W):
            for c in range(C):
                out[c, i] = sec[c, start + i]
                out[C + c, i] = lam[c, start + i]


def finish(par, cx, cr, ct, cf, met, state, sec, lam, re2, ro2, th2, new, adj, lr, hi, lo, tt):
    mt = metric_tile(met)
    evr = is_even(par[1])
    ev8 = evr[:8]
    rx = [-DT * cx[TAPS - 1 - j] for j in range(TAPS)]
    rr = [-DT * cr[TAPS - 1 - j] for j in range(TAPS)]
    rt = [-DT * ct[TAPS - 1 - j] for j in range(TAPS)]
    tc = t_pack_coefs(rt)
    packed = [[t_halo_packed(th2[c, xx], tc) for xx in range(2)] for c in range(C)]

    def fill(k):
        for c in range(C):
            a, b = re2[c, k], ro2[c, k]
            low, high = jnp.where(ev8, b, a), jnp.where(ev8, a, b)
            for xx in range(2):
                x = 2 * k + xx
                value = lam[c, x]
                lr[c, x, 0:8] = low if xx else pltpu.roll(low, 4, 0)
                lr[c, x, 8:24] = value
                lr[c, x, 24:32] = pltpu.roll(high, 4, 0) if xx else high
                hi[x, c], lo[x, c] = split(mt * value)

    loop(0, NX // 2, fill)
    t_own(hi, lo, rt, tt)

    def add(k):
        for c in range(C):
            for xx in range(2):
                tt[2 * k + xx, c] += t_unpack(packed[c][xx], k)

    loop(0, NX // 2, add)
    fcs = [cf[j] for j in range(TAPS)]

    def plane(x):
        q = [state[c, x] for c in range(C)]
        pr = prims(q)
        a, b, g = [], [], []
        for c in range(C):
            a.append(x_taps(lambda at: lam[c, at], x, rx))
            acc = None
            for j in range(TAPS):
                term = rr[j] * lr[c, x, 4 + j : 20 + j]
                acc = term if acc is None else acc + term
            b.append(acc)
            g.append(tt[x, c])
        out = pull(q, pr, a, b, g)
        for c in range(C):
            adj[c, x] = lam[c, x] + out[c]
            new[c, x] = sec[c, x] - x_taps(lambda at: sec[c, at], x, fcs)

    over_planes(plane)


def edges(par, cx, cf, state, xe2, xo2, nin, ain, nout, aout, nb, ab, sems):
    evx = is_even(par[0])
    rx = [-DT * cx[TAPS - 1 - j] for j in range(TAPS)]
    fcs = [cf[j] for j in range(TAPS)]
    starts = (0, NX - W)

    def moves(src, dst, buf, back, first):
        out = []
        for i, at in enumerate(starts):
            if back:
                out.append(pltpu.make_async_copy(buf.at[i], dst.at[:, pl.ds(at, W)], sems.at[first + i]))
            else:
                out.append(pltpu.make_async_copy(src.at[:, pl.ds(at, W)], buf.at[i], sems.at[first + i]))
        return out

    loads = moves(nin, None, nb, False, 0) + moves(ain, None, ab, False, 2)
    for m in loads:
        m.start()
    for m in loads:
        m.wait()
    for side, at in enumerate(starts):
        low = side == 0
        near, far = (xo2, xe2) if low else (xe2, xo2)
        for c in range(C):
            planes = [jnp.where(evx, near[c, i], far[c, i]) for i in range(W)]
            for i in range(W):
                nb[side, c, i] -= x_halo(planes, i, low, fcs)
        halos = [
            [jnp.where(evx, near[C + c, i], far[C + c, i]) for i in range(W)] for c in range(C)
        ]
        for i in range(W):
            q = [state[c, at + i] for c in range(C)]
            a = [x_halo(halos[c], i, low, rx) for c in range(C)]
            out = pull_x(q, prims(q), a)
            for c in range(C):
                ab[side, c, i] += out[c]
    stores = moves(None, nout, nb, True, 0) + moves(None, aout, ab, True, 2)
    for m in stores:
        m.start()
    for m in stores:
        m.wait()


def f32(*shape):
    return jax.ShapeDtypeStruct(shape, F32)


FULL = (C, NX, NR, NT)
XPAY = (2 * C, W, NR, NT)
RPAY = (C, NX // 2, 8, NT)
TPAY = (C, 2, NR, NT)


def call(kernel, ins, outs, scratch=(), out_specs=None, **kw):
    return pl.pallas_call(
        kernel,
        in_specs=ins,
        out_specs=out_specs or [VM] * len(outs),
        out_shape=[f32(*s) for s in outs],
        scratch_shapes=list(scratch),
        name=kernel.__name__,
        **kw,
    )


def swap(value, axis, odd):
    count = lax.axis_size(axis)
    pairs = []
    for i in range(odd, count - 1, 2):
        pairs += [(i, i + 1), (i + 1, i)]
    return lax.ppermute(value, axis, pairs)


def across(value):
    return lax.ppermute(value, "th", [(0, 1), (1, 0)])


SPLIT = [pltpu.VMEM((NX, C, NR, NT), BF16), pltpu.VMEM((NX, C, NR, NT), BF16), pltpu.VMEM((NX, C, NR, NT), F32)]
WIDE_R = pltpu.VMEM((C, NX, 32, NT), F32)


def shards(state, seed, cx, cr, ct, cf, met):
    par = jnp.stack([lax.axis_index("gx") % 2, lax.axis_index("row") % 2]).astype(jnp.int32)
    xe, xo = call(rims_x, [SM, VM, VM], [XPAY, XPAY])(par, state, seed)
    xe, xo = swap(xe, "gx", 0), swap(xo, "gx", 1)
    re, ro, th = call(rims_rt, [SM, VM], [RPAY, RPAY, TPAY])(par, state)
    re, ro, th = swap(re, "row", 0), swap(ro, "row", 1), across(th)
    psec, plam = call(
        own,
        [SM] * 5 + [VM] * 2,
        [FULL, FULL],
        [pltpu.VMEM(FULL, F32), WIDE_R] + SPLIT,
    )(cx, cr, ct, cf, met, state, seed)
    sec, lam, xe2, xo2, re2, ro2, th2 = call(
        join, [SM] * 6 + [VM] * 7, [FULL, FULL, XPAY, XPAY, RPAY, RPAY, TPAY]
    )(par, cx, cr, ct, cf, met, psec, plam, xe, xo, re, ro, th)
    xe2, xo2 = swap(xe2, "gx", 0), swap(xo2, "gx", 1)
    re2, ro2, th2 = swap(re2, "row", 0), swap(ro2, "row", 1), across(th2)
    new, adj = call(
        finish, [SM] * 6 + [VM] * 6, [FULL, FULL], [WIDE_R] + SPLIT
    )(par, cx, cr, ct, cf, met, state, sec, lam, re2, ro2, th2)
    rim = pltpu.VMEM((2, C, W, NR, NT), F32)
    new, adj = call(
        edges,
        [SM] * 3 + [VM] * 3 + [ANY] * 2,
        [FULL, FULL],
        [rim, rim, pltpu.SemaphoreType.DMA((4,))],
        out_specs=[ANY, ANY],
        input_output_aliases={6: 0, 7: 1},
    )(par, cx, cf, state, xe2, xo2, new, adj)
    return new, adj


def solution(mesh):
    whole = P(None, "gx", "row", "th")
    return jax.shard_map(
        shards,
        mesh=mesh,
        in_specs=(whole, whole, P(), P(), P(), P(), P("row")),
        out_specs=(whole, whole),
        check_vma=False,
    )
```

```python
import functools

import jax
import jax.numpy as jnp
from jax import lax
from jax.experimental import pallas as pl
from jax.experimental.pallas import tpu as pltpu
from jax.sharding import PartitionSpec as P


DT = 0.1
GAM = 0.4
W = 4
TAPS = 9
C = 5
NX, NR, NT = 32, 16, 128
F32 = jnp.float32
BF16 = jnp.bfloat16
VM = pl.BlockSpec(memory_space=pltpu.VMEM)
SM = pl.BlockSpec(memory_space=pltpu.SMEM)
ANY = pl.BlockSpec(memory_space=pl.ANY)


def prims(q):
    inv = 1.0 / q[0]
    u, v, w = q[1] * inv, q[2] * inv, q[3] * inv
    p = GAM * (q[4] - 0.5 * (q[1] * u + q[2] * v + q[3] * w))
    return inv, u, v, w, p, q[4] + p


def flux_x(q, pr):
    _, u, _, _, p, h = pr
    return [q[1], q[1] * u + p, q[2] * u, q[3] * u, h * u]


def flux_r(q, pr):
    _, _, v, _, p, h = pr
    return [q[2], q[1] * v, q[2] * v + p, q[3] * v, h * v]


def flux_t(q, pr):
    _, _, _, w, p, h = pr
    return [q[3], q[1] * w, q[2] * w, q[3] * w + p, h * w]


def pull(q, pr, a, b, c):
    inv, u, v, w, _, h = pr
    ub = a[1] * q[1] + a[2] * q[2] + a[3] * q[3] + a[4] * h
    vb = b[1] * q[1] + b[2] * q[2] + b[3] * q[3] + b[4] * h
    wb = c[1] * q[1] + c[2] * q[2] + c[3] * q[3] + c[4] * h
    hb = a[4] * u + b[4] * v + c[4] * w
    pb = a[1] + b[2] + c[3] + hb
    s = (-0.5 * GAM) * pb
    ub = (ub + s * q[1]) * inv
    vb = (vb + s * q[2]) * inv
    wb = (wb + s * q[3]) * inv
    o1 = a[0] + (a[1] + s) * u + b[1] * v + c[1] * w + ub
    o2 = b[0] + a[2] * u + (b[2] + s) * v + c[2] * w + vb
    o3 = c[0] + a[3] * u + b[3] * v + (c[3] + s) * w + wb
    o4 = hb + GAM * pb
    o0 = -(ub * u + vb * v + wb * w)
    return [o0, o1, o2, o3, o4]


def pull_x(q, pr, a):
    inv, u, v, w, _, h = pr
    hb = a[4] * u
    pb = a[1] + hb
    s = (-0.5 * GAM) * pb
    ub = (a[1] * q[1] + a[2] * q[2] + a[3] * q[3] + a[4] * h + s * q[1]) * inv
    vb = s * v
    wb = s * w
    o1 = a[0] + (a[1] + s) * u + ub
    o2 = a[2] * u + s * v + vb
    o3 = a[3] * u + s * w + wb
    o4 = hb + GAM * pb
    o0 = -(ub * u + vb * v + wb * w)
    return [o0, o1, o2, o3, o4]


def iota(shape, dim):
    return lax.broadcasted_iota(jnp.int32, shape, dim)


def metric_tile(met):
    row = iota((NR, NT), 0)
    tile = jnp.zeros((NR, NT), F32)
    for r in range(NR):
        tile = jnp.where(row == r, met[r], tile)
    return tile


def parity(axis):
    return lax.axis_index(axis) % 2


def is_even(axis):
    return jnp.full((NR, NT), parity(axis), jnp.int32) == 0


def split(x):
    hi = x.astype(BF16)
    return hi, (x - hi.astype(F32)).astype(BF16)


def band(coef):
    offset = iota((NT, NT), 0) - iota((NT, NT), 1) + W
    mat = jnp.zeros((NT, NT), F32)
    for j in range(TAPS):
        mat = jnp.where(offset == j, coef[j], mat)
    return mat


def t_own(hi, lo, coef, out):
    bhi, blo = split(band(coef))
    both = jnp.concatenate([bhi, blo], axis=1)
    step = 8
    for g in range(NX // step):
        h = hi[pl.ds(g * step, step)].reshape(step * C * NR, NT)
        l = lo[pl.ds(g * step, step)].reshape(step * C * NR, NT)
        first = jnp.dot(h, both, preferred_element_type=F32)
        second = jnp.dot(l, bhi, preferred_element_type=F32)
        total = first[:, :NT] + first[:, NT:] + second
        out[pl.ds(g * step, step)] = total.reshape(step, C, NR, NT)


def t_pack_coefs(coef):
    lane = iota((NR, NT), 1) % 8
    masks = {}
    for j in range(W):
        masks[j] = jnp.where((lane >= 4) & (lane < 8 - j), coef[j], 0.0)
    for j in range(W + 1, TAPS):
        masks[j] = jnp.where((lane >= 8 - j) & (lane < 4), coef[j], 0.0)
    return masks


def t_halo_packed(rims, masks):
    total = None
    for j, m in masks.items():
        term = m * pltpu.roll(rims, (4 - j) % NT, 1)
        total = term if total is None else total + term
    return total


def t_unpack(packed, k):
    lane = iota((NR, NT), 1)
    moved = pltpu.roll(packed, 124 - 8 * k, 1)
    return jnp.where((lane < 4) | (lane >= 124), moved, 0.0)


def t_pack_into(ref, fields, xx, k):
    lane = iota((NR, NT), 1)
    for c in range(C):
        moved = pltpu.roll(fields[c], 8 * k + 4, 1)
        ref[c, xx] = jnp.where(lane // 8 == k, moved, ref[c, xx])


def r_pack(first, second, even):
    sub = iota((8, NT), 0)
    low = jnp.where(sub < 4, first[:8], pltpu.roll(second[:8], 4, 0))
    high = jnp.where(sub < 4, pltpu.roll(first[8:], 4, 0), second[8:])
    ev = even[:8]
    return jnp.where(ev, high, low), jnp.where(ev, low, high)


def r_coefs(coef):
    sub = iota((8, NT), 0)
    low = [jnp.where(sub < 4 - j, coef[j], 0.0) for j in range(W)]
    high = {j: jnp.where(sub >= 12 - j, coef[j], 0.0) for j in range(W + 1, TAPS)}
    return low, high


def r_halo(low, high, xx, coefs):
    lo_c, hi_c = coefs
    top = None
    for j in range(W):
        shift = (8 - (4 * xx + j)) % 8
        term = lo_c[j] * (pltpu.roll(low, shift, 0) if shift else low)
        top = term if top is None else top + term
    bottom = None
    for j in range(W + 1, TAPS):
        shift = (12 - j - 4 * xx) % 8
        term = hi_c[j] * (pltpu.roll(high, shift, 0) if shift else high)
        bottom = term if bottom is None else bottom + term
    return jnp.concatenate([top, bottom], axis=0)


def x_taps(read, x, coef):
    total = None
    for j in range(TAPS):
        at = x + j - W
        if isinstance(x, int) and not 0 <= at < NX:
            continue
        term = coef[j] * read(at)
        total = term if total is None else total + term
    return total


def x_halo(planes, i, low, coef):
    total = None
    for j in range(TAPS):
        at = i + j if low else i + j - 8
        if not 0 <= at < W:
            continue
        term = coef[j] * planes[at]
        total = term if total is None else total + term
    return total


def over_planes(body):
    for x in range(W):
        body(x)

    def step(x, carry):
        body(x)
        return carry

    lax.fori_loop(W, NX - W, step, 0)
    for x in range(NX - W, NX):
        body(x)


def loop(lo, hi, body):
    def step(k, carry):
        body(k)
        return carry

    lax.fori_loop(lo, hi, step, 0)


def rims_x(state, seed, xe, xo):
    even = parity("gx") == 0
    first = jnp.where(even, NX - W, 0)
    second = jnp.where(even, 0, NX - W)
    for start, out in ((first, xe), (second, xo)):
        for i in range(W):
            q = [state[c, start + i] for c in range(C)]
            f = flux_x(q, prims(q))
            for c in range(C):
                out[c, i] = f[c]
                out[C + c, i] = seed[c, start + i]


def rims_rt(state, re, ro, th):
    even = is_even("row")
    th[...] = jnp.zeros(th.shape, F32)

    def pair(k):
        keep = []
        for xx in range(2):
            q = [state[c, 2 * k + xx] for c in range(C)]
            pr = prims(q)
            keep.append(flux_r(q, pr))
            t_pack_into(th, flux_t(q, pr), xx, k)
        for c in range(C):
            re[c, k], ro[c, k] = r_pack(keep[0][c], keep[1][c], even)

    loop(0, NX // 2, pair)


def own(cx, cr, ct, cf, met, state, seed, psec, plam, fx, fr, hi, lo, tt):
    mt = metric_tile(met)
    zero = jnp.zeros((8, NT), F32)

    def fill(x):
        q = [state[c, x] for c in range(C)]
        pr = prims(q)
        f, g, h = flux_x(q, pr), flux_r(q, pr), flux_t(q, pr)
        for c in range(C):
            fx[c, x] = f[c]
            fr[c, x, 0:8] = zero
            fr[c, x, 8:24] = g[c]
            fr[c, x, 24:32] = zero
            hi[x, c], lo[x, c] = split(h[c])

    loop(0, NX, fill)
    t_own(hi, lo, ct, tt)
    fc = [cf[TAPS - 1 - j] for j in range(TAPS)]
    xc = [cx[j] for j in range(TAPS)]

    def plane(x):
        for c in range(C):
            acc = x_taps(lambda at: fx[c, at], x, xc) + mt * tt[x, c]
            for j in range(TAPS):
                acc += cr[j] * fr[c, x, 4 + j : 20 + j]
            psec[c, x] = state[c, x] - DT * acc
            plam[c, x] = seed[c, x] - x_taps(lambda at: seed[c, at], x, fc)

    over_planes(plane)


def join(cx, cr, ct, cf, met, psec, plam, xe, xo, re, ro, th, sec, lam, xe2, xo2, re2, ro2, th2):
    mt = metric_tile(met)
    evx, evr = is_even("gx"), is_even("row")
    fc = [cf[TAPS - 1 - j] for j in range(TAPS)]
    xc = [cx[j] for j in range(TAPS)]
    for low in (True, False):
        base = 0 if low else NX - W
        for c in range(2 * C):
            near, far = (xo, xe) if low else (xe, xo)
            planes = [jnp.where(evx, near[c, i], far[c, i]) for i in range(W)]
            for i in range(W):
                if c < C:
                    sec[c, base + i] = psec[c, base + i] - DT * x_halo(planes, i, low, xc)
                else:
                    lam[c - C, base + i] = plam[c - C, base + i] - x_halo(planes, i, low, fc)
    th2[...] = jnp.zeros(th2.shape, F32)
    rc = r_coefs(cr)
    tc = t_pack_coefs(ct)
    packed = [[mt * t_halo_packed(th[c, xx], tc) for xx in range(2)] for c in range(C)]
    ev8 = evr[:8]

    def pair(k, s_ref, l_ref):
        lams = [[], []]
        for c in range(C):
            a, b = re[c, k], ro[c, k]
            low, high = jnp.where(ev8, b, a), jnp.where(ev8, a, b)
            for xx in range(2):
                x = 2 * k + xx
                share = r_halo(low, high, xx, rc) + t_unpack(packed[c][xx], k)
                sec[c, x] = s_ref[c, x] - DT * share
                value = l_ref[c, x]
                lam[c, x] = value
                lams[xx].append(value)
        for c in range(C):
            re2[c, k], ro2[c, k] = r_pack(lams[0][c], lams[1][c], evr)
        for xx in range(2):
            t_pack_into(th2, [mt * v for v in lams[xx]], xx, k)

    loop(0, 2, functools.partial(pair, s_ref=sec, l_ref=lam))
    loop(2, 14, functools.partial(pair, s_ref=psec, l_ref=plam))
    loop(14, 16, functools.partial(pair, s_ref=sec, l_ref=lam))
    even = parity("gx") == 0
    first = jnp.where(even, NX - W, 0)
    second = jnp.where(even, 0, NX - W)
    for start, out in ((first, xe2), (second, xo2)):
        for i in range(W):
            for c in range(C):
                out[c, i] = sec[c, start + i]
                out[C + c, i] = lam[c, start + i]


def finish(cx, cr, ct, cf, met, state, sec, lam, re2, ro2, th2, new, adj, nrim, arim, lr, hi, lo, tt, nb, ab, sems):
    mt = metric_tile(met)
    evr = is_even("row")
    ev8 = evr[:8]
    rx = [-DT * cx[TAPS - 1 - j] for j in range(TAPS)]
    rr = [-DT * cr[TAPS - 1 - j] for j in range(TAPS)]
    rt = [-DT * ct[TAPS - 1 - j] for j in range(TAPS)]
    tc = t_pack_coefs(rt)
    packed = [[t_halo_packed(th2[c, xx], tc) for xx in range(2)] for c in range(C)]

    def fill(k):
        for c in range(C):
            a, b = re2[c, k], ro2[c, k]
            low, high = jnp.where(ev8, b, a), jnp.where(ev8, a, b)
            for xx in range(2):
                x = 2 * k + xx
                value = lam[c, x]
                lr[c, x, 0:8] = low if xx else pltpu.roll(low, 4, 0)
                lr[c, x, 8:24] = value
                lr[c, x, 24:32] = pltpu.roll(high, 4, 0) if xx else high
                hi[x, c], lo[x, c] = split(mt * value)

    loop(0, NX // 2, fill)
    t_own(hi, lo, rt, tt)

    def add(k):
        for c in range(C):
            for xx in range(2):
                tt[2 * k + xx, c] += t_unpack(packed[c][xx], k)

    loop(0, NX // 2, add)
    fcs = [cf[j] for j in range(TAPS)]

    def plane(x):
        q = [state[c, x] for c in range(C)]
        pr = prims(q)
        a, b, g = [], [], []
        for c in range(C):
            a.append(x_taps(lambda at: lam[c, at], x, rx))
            acc = None
            for j in range(TAPS):
                term = rr[j] * lr[c, x, 4 + j : 20 + j]
                acc = term if acc is None else acc + term
            b.append(acc)
            g.append(tt[x, c])
        out = pull(q, pr, a, b, g)
        for c in range(C):
            av = lam[c, x] + out[c]
            nv = sec[c, x] - x_taps(lambda at: sec[c, at], x, fcs)
            if isinstance(x, int):
                side, at = (0, x) if x < W else (1, x - NX + W)
                arim[side, c, at], nrim[side, c, at] = av, nv
            else:
                ab[c, x - W], nb[c, x - W] = av, nv

    lax.fori_loop(W, NX - W, lambda x, carry: (plane(x), carry)[1], 0)
    inside = pl.ds(W, NX - 2 * W)
    moves = [
        pltpu.make_async_copy(ab, adj.at[:, inside], sems.at[0]),
        pltpu.make_async_copy(nb, new.at[:, inside], sems.at[1]),
    ]
    for move in moves:
        move.start()
    for x in (*range(W), *range(NX - W, NX)):
        plane(x)
    for move in moves:
        move.wait()


def edges(cx, cf, state, xe2, xo2, nrim, arim, nin, ain, nout, aout, nb, ab, sems):
    evx = is_even("gx")
    rx = [-DT * cx[TAPS - 1 - j] for j in range(TAPS)]
    fcs = [cf[j] for j in range(TAPS)]
    starts = (0, NX - W)
    moves = []

    def put(buf, dst, side, slot):
        move = pltpu.make_async_copy(
            buf.at[side], dst.at[:, pl.ds(starts[side], W)], sems.at[slot + side]
        )
        move.start()
        moves.append(move)

    for side, at in enumerate(starts):
        low = side == 0
        mine, other = (xo2, xe2) if low else (xe2, xo2)
        for i in range(W):
            q = [state[c, at + i] for c in range(C)]
            a = []
            for c in range(C):
                planes = [jnp.where(evx, mine[C + c, h], other[C + c, h]) for h in range(W)]
                a.append(x_halo(planes, i, low, rx))
            out = pull_x(q, prims(q), a)
            for c in range(C):
                ab[side, c, i] = arim[side, c, i] + out[c]
        put(ab, aout, side, 2)
        for c in range(C):
            planes = [jnp.where(evx, mine[c, i], other[c, i]) for i in range(W)]
            for i in range(W):
                nb[side, c, i] = nrim[side, c, i] - x_halo(planes, i, low, fcs)
        put(nb, nout, side, 0)
    for move in moves:
        move.wait()


def near(value):
    return pltpu.with_memory_space_constraint(value, pltpu.VMEM)


LIMIT = pltpu.CompilerParams(vmem_limit_bytes=24 << 20)
FULL = (C, NX, NR, NT)
XPAY = (2 * C, W, NR, NT)
RPAY = (C, NX // 2, 8, NT)
TPAY = (C, 2, NR, NT)


def call(kernel, smem, vmem, outs, scratch=()):
    run = pl.pallas_call(
        kernel,
        in_specs=[SM] * len(smem) + [VM] * len(vmem),
        out_specs=[VM] * len(outs),
        out_shape=[pltpu.VMEM(s, F32) for s in outs],
        scratch_shapes=list(scratch),
        compiler_params=LIMIT,
    )
    return run(*smem, *[near(v) for v in vmem])


def swap(value, axis, odd):
    count = lax.axis_size(axis)
    pairs = []
    for i in range(odd, count - 1, 2):
        pairs += [(i, i + 1), (i + 1, i)]
    return lax.ppermute(value, axis, pairs)


def across(value):
    return lax.ppermute(value, "th", [(0, 1), (1, 0)])


SPLIT = [pltpu.VMEM((NX, C, NR, NT), BF16), pltpu.VMEM((NX, C, NR, NT), BF16), pltpu.VMEM((NX, C, NR, NT), F32)]
WIDE_R = pltpu.VMEM((C, NX, 32, NT), F32)


def shards(state, seed, cx, cr, ct, cf, met):
    xe, xo = call(rims_x, [], [state, seed], [XPAY, XPAY])
    xe, xo = swap(xe, "gx", 0), swap(xo, "gx", 1)
    re, ro, th = call(rims_rt, [], [state], [RPAY, RPAY, TPAY])
    re, ro, th = swap(re, "row", 0), swap(ro, "row", 1), across(th)
    psec, plam = call(
        own,
        [cx, cr, ct, cf, met],
        [state, seed],
        [FULL, FULL],
        [pltpu.VMEM(FULL, F32), WIDE_R] + SPLIT,
    )
    sec, lam, xe2, xo2, re2, ro2, th2 = call(
        join,
        [cx, cr, ct, cf, met],
        [psec, plam, xe, xo, re, ro, th],
        [FULL, FULL, XPAY, XPAY, RPAY, RPAY, TPAY],
    )
    th2 = across(th2)
    re2 = swap(re2, "row", 0)
    ro2 = swap(ro2, "row", 1)
    xe2 = swap(xe2, "gx", 0)
    xo2 = swap(xo2, "gx", 1)
    rim = (2, C, W, NR, NT)
    inner = pltpu.VMEM((C, NX - 2 * W, NR, NT), F32)
    whole = jax.ShapeDtypeStruct(FULL, F32)
    new, adj, nrim, arim = pl.pallas_call(
        finish,
        in_specs=[SM] * 5 + [VM] * 6,
        out_specs=[ANY, ANY, VM, VM],
        out_shape=[whole, whole, pltpu.VMEM(rim, F32), pltpu.VMEM(rim, F32)],
        scratch_shapes=[WIDE_R] + SPLIT + [inner, inner, pltpu.SemaphoreType.DMA((2,))],
        name="finish",
        compiler_params=LIMIT,
    )(cx, cr, ct, cf, met, *map(near, (state, sec, lam, re2, ro2, th2)))
    return pl.pallas_call(
        edges,
        in_specs=[SM] * 2 + [VM] * 5 + [ANY] * 2,
        out_specs=[ANY, ANY],
        out_shape=[whole, whole],
        scratch_shapes=[pltpu.VMEM(rim, F32), pltpu.VMEM(rim, F32), pltpu.SemaphoreType.DMA((4,))],
        input_output_aliases={7: 0, 8: 1},
        name="edges",
        compiler_params=LIMIT,
    )(cx, cf, *map(near, (state, xe2, xo2, nrim, arim)), new, adj)


def solution(mesh):
    whole = P(None, "gx", "row", "th")

    return jax.shard_map(
        shards,
        mesh=mesh,
        in_specs=(whole, whole, P(), P(), P(), P(), P("row")),
        out_specs=(whole, whole),
        check_vma=False,
    )
```

```python
import functools

import jax
import jax.numpy as jnp
from jax import lax
from jax.experimental import pallas as pl
from jax.experimental.pallas import tpu as pltpu
from jax.sharding import PartitionSpec as P


DT = 0.1
GAM = 0.4
W = 4
TAPS = 9
C = 5
NX, NR, NT = 32, 16, 128
F32 = jnp.float32
BF16 = jnp.bfloat16
VM = pl.BlockSpec(memory_space=pltpu.VMEM)
SM = pl.BlockSpec(memory_space=pltpu.SMEM)
ANY = pl.BlockSpec(memory_space=pl.ANY)


def prims(q):
    inv = 1.0 / q[0]
    u, v, w = q[1] * inv, q[2] * inv, q[3] * inv
    p = GAM * (q[4] - 0.5 * (q[1] * u + q[2] * v + q[3] * w))
    return inv, u, v, w, p, q[4] + p


def flux_x(q, pr):
    _, u, _, _, p, h = pr
    return [q[1], q[1] * u + p, q[2] * u, q[3] * u, h * u]


def flux_r(q, pr):
    _, _, v, _, p, h = pr
    return [q[2], q[1] * v, q[2] * v + p, q[3] * v, h * v]


def flux_t(q, pr):
    _, _, _, w, p, h = pr
    return [q[3], q[1] * w, q[2] * w, q[3] * w + p, h * w]


def pull(q, pr, a, b, c):
    inv, u, v, w, _, h = pr
    ub = a[1] * q[1] + a[2] * q[2] + a[3] * q[3] + a[4] * h
    vb = b[1] * q[1] + b[2] * q[2] + b[3] * q[3] + b[4] * h
    wb = c[1] * q[1] + c[2] * q[2] + c[3] * q[3] + c[4] * h
    hb = a[4] * u + b[4] * v + c[4] * w
    pb = a[1] + b[2] + c[3] + hb
    s = (-0.5 * GAM) * pb
    ub = (ub + s * q[1]) * inv
    vb = (vb + s * q[2]) * inv
    wb = (wb + s * q[3]) * inv
    o1 = a[0] + (a[1] + s) * u + b[1] * v + c[1] * w + ub
    o2 = b[0] + a[2] * u + (b[2] + s) * v + c[2] * w + vb
    o3 = c[0] + a[3] * u + b[3] * v + (c[3] + s) * w + wb
    o4 = hb + GAM * pb
    o0 = -(ub * u + vb * v + wb * w)
    return [o0, o1, o2, o3, o4]


def pull_x(q, pr, a):
    inv, u, v, w, _, h = pr
    hb = a[4] * u
    pb = a[1] + hb
    s = (-0.5 * GAM) * pb
    ub = (a[1] * q[1] + a[2] * q[2] + a[3] * q[3] + a[4] * h + s * q[1]) * inv
    vb = s * v
    wb = s * w
    o1 = a[0] + (a[1] + s) * u + ub
    o2 = a[2] * u + s * v + vb
    o3 = a[3] * u + s * w + wb
    o4 = hb + GAM * pb
    o0 = -(ub * u + vb * v + wb * w)
    return [o0, o1, o2, o3, o4]


def iota(shape, dim):
    return lax.broadcasted_iota(jnp.int32, shape, dim)


def metric_tile(met):
    row = iota((NR, NT), 0)
    tile = jnp.zeros((NR, NT), F32)
    for r in range(NR):
        tile = jnp.where(row == r, met[r], tile)
    return tile


def parity(axis):
    return lax.axis_index(axis) % 2


def is_even(axis):
    return jnp.full((NR, NT), parity(axis), jnp.int32) == 0


def split(x):
    hi = x.astype(BF16)
    return hi, (x - hi.astype(F32)).astype(BF16)


def band(coef):
    offset = iota((NT, NT), 0) - iota((NT, NT), 1) + W
    mat = jnp.zeros((NT, NT), F32)
    for j in range(TAPS):
        mat = jnp.where(offset == j, coef[j], mat)
    return mat


def t_own(hi, lo, coef, out):
    bhi, blo = split(band(coef))
    mat = jnp.concatenate([bhi, bhi, blo], axis=0)
    step = 8
    for g in range(NX // step):
        h = hi[pl.ds(g * step, step)].reshape(step * C * NR, NT)
        l = lo[pl.ds(g * step, step)].reshape(step * C * NR, NT)
        total = jnp.dot(jnp.concatenate([h, l, h], axis=1), mat, preferred_element_type=F32)
        out[pl.ds(g * step, step)] = total.reshape(step, C, NR, NT)


def t_pack_coefs(coef):
    lane = iota((NR, NT), 1) % 8
    masks = {}
    for j in range(W):
        masks[j] = jnp.where((lane >= 4) & (lane < 8 - j), coef[j], 0.0)
    for j in range(W + 1, TAPS):
        masks[j] = jnp.where((lane >= 8 - j) & (lane < 4), coef[j], 0.0)
    return masks


def t_halo_packed(rims, masks):
    total = None
    for j, m in masks.items():
        term = m * pltpu.roll(rims, (4 - j) % NT, 1)
        total = term if total is None else total + term
    return total


def t_unpack(packed, k):
    lane = iota((NR, NT), 1)
    moved = pltpu.roll(packed, 124 - 8 * k, 1)
    return jnp.where((lane < 4) | (lane >= 124), moved, 0.0)


def t_pack_into(ref, fields, xx, k):
    lane = iota((NR, NT), 1)
    for c in range(C):
        moved = pltpu.roll(fields[c], 8 * k + 4, 1)
        ref[c, xx] = jnp.where(lane // 8 == k, moved, ref[c, xx])


def r_pack(first, second, even):
    sub = iota((8, NT), 0)
    low = jnp.where(sub < 4, first[:8], pltpu.roll(second[:8], 4, 0))
    high = jnp.where(sub < 4, pltpu.roll(first[8:], 4, 0), second[8:])
    ev = even[:8]
    return jnp.where(ev, high, low), jnp.where(ev, low, high)


def r_coefs(coef):
    sub = iota((8, NT), 0)
    low = [jnp.where(sub < 4 - j, coef[j], 0.0) for j in range(W)]
    high = {j: jnp.where(sub >= 12 - j, coef[j], 0.0) for j in range(W + 1, TAPS)}
    return low, high


def r_halo(low, high, xx, coefs):
    lo_c, hi_c = coefs
    top = None
    for j in range(W):
        shift = (8 - (4 * xx + j)) % 8
        term = lo_c[j] * (pltpu.roll(low, shift, 0) if shift else low)
        top = term if top is None else top + term
    bottom = None
    for j in range(W + 1, TAPS):
        shift = (12 - j - 4 * xx) % 8
        term = hi_c[j] * (pltpu.roll(high, shift, 0) if shift else high)
        bottom = term if bottom is None else bottom + term
    return jnp.concatenate([top, bottom], axis=0)


def x_taps(read, x, coef):
    total = None
    for j in range(TAPS):
        at = x + j - W
        if isinstance(x, int) and not 0 <= at < NX:
            continue
        term = coef[j] * read(at)
        total = term if total is None else total + term
    return total


def x_halo(planes, i, low, coef):
    total = None
    for j in range(TAPS):
        at = i + j if low else i + j - 8
        if not 0 <= at < W:
            continue
        term = coef[j] * planes[at]
        total = term if total is None else total + term
    return total


def over_planes(body):
    for x in range(W):
        body(x)

    def step(x, carry):
        body(x)
        return carry

    lax.fori_loop(W, NX - W, step, 0)
    for x in range(NX - W, NX):
        body(x)


def loop(lo, hi, body, unroll=1):
    def step(k, carry):
        body(k)
        return carry

    lax.fori_loop(lo, hi, step, 0, unroll=unroll)


def rims(state_hbm, seed_hbm, state, seed, xe, xo, re, ro, th, sems):
    moves = [
        pltpu.make_async_copy(state_hbm, state, sems.at[0]),
        pltpu.make_async_copy(seed_hbm, seed, sems.at[1]),
    ]
    for move in moves:
        move.start()
    th[...] = jnp.zeros(th.shape, F32)
    even_r = is_even("row")
    even = parity("gx") == 0
    first = jnp.where(even, NX - W, 0)
    second = jnp.where(even, 0, NX - W)
    moves[0].wait()

    def pair(k):
        keep = []
        for xx in range(2):
            q = [state[c, 2 * k + xx] for c in range(C)]
            pr = prims(q)
            keep.append(flux_r(q, pr))
            t_pack_into(th, flux_t(q, pr), xx, k)
        for c in range(C):
            re[c, k], ro[c, k] = r_pack(keep[0][c], keep[1][c], even_r)

    loop(0, NX // 2, pair, 2)
    for start, out in ((first, xe), (second, xo)):
        for i in range(W):
            q = [state[c, start + i] for c in range(C)]
            f = flux_x(q, prims(q))
            for c in range(C):
                out[c, i] = f[c]
    moves[1].wait()
    for start, out in ((first, xe), (second, xo)):
        for i in range(W):
            for c in range(C):
                out[C + c, i] = seed[c, start + i]


def own(cx, cr, ct, cf, met, state, seed, psec, plam, fx, fr, hi, lo, tt):
    mt = metric_tile(met)
    zero = jnp.zeros((8, NT), F32)

    def fill(x):
        q = [state[c, x] for c in range(C)]
        pr = prims(q)
        f, g, h = flux_x(q, pr), flux_r(q, pr), flux_t(q, pr)
        for c in range(C):
            fx[c, x] = f[c]
            fr[c, x, 0:8] = zero
            fr[c, x, 8:24] = g[c]
            fr[c, x, 24:32] = zero
            hi[x, c], lo[x, c] = split(h[c])

    loop(0, NX, fill)
    t_own(hi, lo, [-DT * ct[j] for j in range(TAPS)], tt)
    fc = [-cf[TAPS - 1 - j] for j in range(TAPS)]
    xc = [-DT * cx[j] for j in range(TAPS)]
    rc = [-DT * cr[j] for j in range(TAPS)]

    def plane(x):
        for c in range(C):
            acc = state[c, x] + mt * tt[x, c]
            acc += x_taps(lambda at: fx[c, at], x, xc)
            for j in range(TAPS):
                acc += rc[j] * fr[c, x, 4 + j : 20 + j]
            psec[c, x] = acc
            plam[c, x] = seed[c, x] + x_taps(lambda at: seed[c, at], x, fc)

    over_planes(plane)


def join(cx, cr, ct, cf, met, psec, plam, xe, xo, re, ro, th, sec, lam, xe2, xo2, re2, ro2, th2):
    mt = metric_tile(met)
    evx, evr = is_even("gx"), is_even("row")
    fc = [cf[TAPS - 1 - j] for j in range(TAPS)]
    xc = [cx[j] for j in range(TAPS)]
    for low in (True, False):
        base = 0 if low else NX - W
        for c in range(2 * C):
            near, far = (xo, xe) if low else (xe, xo)
            planes = [jnp.where(evx, near[c, i], far[c, i]) for i in range(W)]
            for i in range(W):
                if c < C:
                    sec[c, base + i] = psec[c, base + i] - DT * x_halo(planes, i, low, xc)
                else:
                    lam[c - C, base + i] = plam[c - C, base + i] - x_halo(planes, i, low, fc)
    th2[...] = jnp.zeros(th2.shape, F32)
    rc = r_coefs(cr)
    tc = t_pack_coefs(ct)
    packed = [[mt * t_halo_packed(th[c, xx], tc) for xx in range(2)] for c in range(C)]
    ev8 = evr[:8]

    def pair(k, s_ref, l_ref):
        lams = [[], []]
        for c in range(C):
            a, b = re[c, k], ro[c, k]
            low, high = jnp.where(ev8, b, a), jnp.where(ev8, a, b)
            for xx in range(2):
                x = 2 * k + xx
                share = r_halo(low, high, xx, rc) + t_unpack(packed[c][xx], k)
                sec[c, x] = s_ref[c, x] - DT * share
                value = l_ref[c, x]
                lam[c, x] = value
                lams[xx].append(value)
        for c in range(C):
            re2[c, k], ro2[c, k] = r_pack(lams[0][c], lams[1][c], evr)
        for xx in range(2):
            t_pack_into(th2, [mt * v for v in lams[xx]], xx, k)

    loop(0, 2, functools.partial(pair, s_ref=sec, l_ref=lam))
    loop(2, 14, functools.partial(pair, s_ref=psec, l_ref=plam))
    loop(14, 16, functools.partial(pair, s_ref=sec, l_ref=lam))
    even = parity("gx") == 0
    first = jnp.where(even, NX - W, 0)
    second = jnp.where(even, 0, NX - W)
    for start, out in ((first, xe2), (second, xo2)):
        for i in range(W):
            for c in range(C):
                out[c, i] = sec[c, start + i]
                out[C + c, i] = lam[c, start + i]


def finish(cx, cr, ct, cf, met, state, sec, lam, re2, ro2, th2, new, adj, nrim, arim, lr, hi, lo, tt, nb, ab, sems):
    mt = metric_tile(met)
    evr = is_even("row")
    ev8 = evr[:8]
    rx = [-DT * cx[TAPS - 1 - j] for j in range(TAPS)]
    rr = [-DT * cr[TAPS - 1 - j] for j in range(TAPS)]
    rt = [-DT * ct[TAPS - 1 - j] for j in range(TAPS)]
    tc = t_pack_coefs(rt)
    packed = [[t_halo_packed(th2[c, xx], tc) for xx in range(2)] for c in range(C)]

    def fill(k):
        for c in range(C):
            a, b = re2[c, k], ro2[c, k]
            low, high = jnp.where(ev8, b, a), jnp.where(ev8, a, b)
            for xx in range(2):
                x = 2 * k + xx
                value = lam[c, x]
                lr[c, x, 0:8] = low if xx else pltpu.roll(low, 4, 0)
                lr[c, x, 8:24] = value
                lr[c, x, 24:32] = pltpu.roll(high, 4, 0) if xx else high
                hi[x, c], lo[x, c] = split(mt * value)

    loop(0, NX // 2, fill)
    t_own(hi, lo, rt, tt)

    def add(k):
        for c in range(C):
            for xx in range(2):
                tt[2 * k + xx, c] += t_unpack(packed[c][xx], k)

    loop(0, NX // 2, add)
    fcs = [cf[j] for j in range(TAPS)]

    def plane(x):
        q = [state[c, x] for c in range(C)]
        pr = prims(q)
        a, b, g = [], [], []
        for c in range(C):
            a.append(x_taps(lambda at: lam[c, at], x, rx))
            acc = None
            for j in range(TAPS):
                term = rr[j] * lr[c, x, 4 + j : 20 + j]
                acc = term if acc is None else acc + term
            b.append(acc)
            g.append(tt[x, c])
        out = pull(q, pr, a, b, g)
        for c in range(C):
            av = lam[c, x] + out[c]
            nv = sec[c, x] - x_taps(lambda at: sec[c, at], x, fcs)
            if isinstance(x, int):
                side, at = (0, x) if x < W else (1, x - NX + W)
                arim[side, c, at], nrim[side, c, at] = av, nv
            else:
                ab[c, x - W], nb[c, x - W] = av, nv

    lax.fori_loop(W, NX - W, lambda x, carry: (plane(x), carry)[1], 0)
    inside = pl.ds(W, NX - 2 * W)
    moves = [
        pltpu.make_async_copy(ab, adj.at[:, inside], sems.at[0]),
        pltpu.make_async_copy(nb, new.at[:, inside], sems.at[1]),
    ]
    for move in moves:
        move.start()
    for x in (*range(W), *range(NX - W, NX)):
        plane(x)
    for move in moves:
        move.wait()


def edges(cx, cf, state, xe2, xo2, nrim, arim, nin, ain, nout, aout, nb, ab, sems):
    evx = is_even("gx")
    rx = [-DT * cx[TAPS - 1 - j] for j in range(TAPS)]
    fcs = [cf[j] for j in range(TAPS)]
    starts = (0, NX - W)
    moves = []

    def put(buf, dst, side, slot):
        move = pltpu.make_async_copy(
            buf.at[side], dst.at[:, pl.ds(starts[side], W)], sems.at[slot + side]
        )
        move.start()
        moves.append(move)

    for side, at in enumerate(starts):
        low = side == 0
        mine, other = (xo2, xe2) if low else (xe2, xo2)
        for i in range(W):
            q = [state[c, at + i] for c in range(C)]
            a = []
            for c in range(C):
                planes = [jnp.where(evx, mine[C + c, h], other[C + c, h]) for h in range(W)]
                a.append(x_halo(planes, i, low, rx))
            out = pull_x(q, prims(q), a)
            for c in range(C):
                ab[side, c, i] = arim[side, c, i] + out[c]
        put(ab, aout, side, 2)
        for c in range(C):
            planes = [jnp.where(evx, mine[c, i], other[c, i]) for i in range(W)]
            for i in range(W):
                nb[side, c, i] = nrim[side, c, i] - x_halo(planes, i, low, fcs)
        put(nb, nout, side, 0)
    for move in moves:
        move.wait()


def near(value):
    return pltpu.with_memory_space_constraint(value, pltpu.VMEM)


LIMIT = pltpu.CompilerParams(vmem_limit_bytes=24 << 20)
FULL = (C, NX, NR, NT)
XPAY = (2 * C, W, NR, NT)
RPAY = (C, NX // 2, 8, NT)
TPAY = (C, 2, NR, NT)


def call(kernel, smem, vmem, outs, scratch=()):
    run = pl.pallas_call(
        kernel,
        in_specs=[SM] * len(smem) + [VM] * len(vmem),
        out_specs=[VM] * len(outs),
        out_shape=[pltpu.VMEM(s, F32) for s in outs],
        scratch_shapes=list(scratch),
        compiler_params=LIMIT,
    )
    return run(*smem, *[near(v) for v in vmem])


def swap(value, axis, odd):
    count = lax.axis_size(axis)
    pairs = []
    for i in range(odd, count - 1, 2):
        pairs += [(i, i + 1), (i + 1, i)]
    return lax.ppermute(value, axis, pairs)


def across(value):
    return lax.ppermute(value, "th", [(0, 1), (1, 0)])


SPLIT = [pltpu.VMEM((NX, C, NR, NT), BF16), pltpu.VMEM((NX, C, NR, NT), BF16), pltpu.VMEM((NX, C, NR, NT), F32)]
WIDE_R = pltpu.VMEM((C, NX, 32, NT), F32)


def shards(state, seed, cx, cr, ct, cf, met):
    shapes = [FULL, FULL, XPAY, XPAY, RPAY, RPAY, TPAY]
    state, seed, xe, xo, re, ro, th = pl.pallas_call(
        rims,
        in_specs=[pl.BlockSpec(memory_space=pltpu.HBM)] * 2,
        out_specs=[VM] * len(shapes),
        out_shape=[pltpu.VMEM(s, F32) for s in shapes],
        scratch_shapes=[pltpu.SemaphoreType.DMA((2,))],
        name="rims",
        compiler_params=LIMIT,
    )(*[pltpu.with_memory_space_constraint(v, pltpu.HBM) for v in (state, seed)])
    th = across(th)
    xe = swap(xe, "gx", 0)
    xo = swap(xo, "gx", 1)
    re = swap(re, "row", 0)
    ro = swap(ro, "row", 1)
    psec, plam = call(
        own,
        [cx, cr, ct, cf, met],
        [state, seed],
        [FULL, FULL],
        [pltpu.VMEM(FULL, F32), WIDE_R] + SPLIT,
    )
    sec, lam, xe2, xo2, re2, ro2, th2 = call(
        join,
        [cx, cr, ct, cf, met],
        [psec, plam, xe, xo, re, ro, th],
        [FULL, FULL, XPAY, XPAY, RPAY, RPAY, TPAY],
    )
    th2 = across(th2)
    re2 = swap(re2, "row", 0)
    ro2 = swap(ro2, "row", 1)
    xe2 = swap(xe2, "gx", 0)
    xo2 = swap(xo2, "gx", 1)
    rim = (2, C, W, NR, NT)
    inner = pltpu.VMEM((C, NX - 2 * W, NR, NT), F32)
    whole = jax.ShapeDtypeStruct(FULL, F32)
    new, adj, nrim, arim = pl.pallas_call(
        finish,
        in_specs=[SM] * 5 + [VM] * 6,
        out_specs=[ANY, ANY, VM, VM],
        out_shape=[whole, whole, pltpu.VMEM(rim, F32), pltpu.VMEM(rim, F32)],
        scratch_shapes=[WIDE_R] + SPLIT + [inner, inner, pltpu.SemaphoreType.DMA((2,))],
        name="finish",
        compiler_params=LIMIT,
    )(cx, cr, ct, cf, met, *map(near, (state, sec, lam, re2, ro2, th2)))
    return pl.pallas_call(
        edges,
        in_specs=[SM] * 2 + [VM] * 5 + [ANY] * 2,
        out_specs=[ANY, ANY],
        out_shape=[whole, whole],
        scratch_shapes=[pltpu.VMEM(rim, F32), pltpu.VMEM(rim, F32), pltpu.SemaphoreType.DMA((4,))],
        input_output_aliases={7: 0, 8: 1},
        name="edges",
        compiler_params=LIMIT,
    )(cx, cf, *map(near, (state, xe2, xo2, nrim, arim)), new, adj)


def solution(mesh):
    whole = P(None, "gx", "row", "th")

    return jax.shard_map(
        shards,
        mesh=mesh,
        in_specs=(whole, whole, P(), P(), P(), P(), P("row")),
        out_specs=(whole, whole),
        check_vma=False,
    )
```

```python
import functools

import jax
import jax.numpy as jnp
from jax import lax
from jax.experimental import pallas as pl
from jax.experimental.pallas import tpu as pltpu
from jax.sharding import PartitionSpec as P


DT = 0.1
GAM = 0.4
W = 4
TAPS = 9
C = 5
NX, NR, NT = 32, 16, 128
F32 = jnp.float32
BF16 = jnp.bfloat16
VM = pl.BlockSpec(memory_space=pltpu.VMEM)
SM = pl.BlockSpec(memory_space=pltpu.SMEM)
ANY = pl.BlockSpec(memory_space=pl.ANY)


def prims(q):
    inv = 1.0 / q[0]
    u, v, w = q[1] * inv, q[2] * inv, q[3] * inv
    p = GAM * (q[4] - 0.5 * (q[1] * u + q[2] * v + q[3] * w))
    return inv, u, v, w, p, q[4] + p


def flux_x(q, pr):
    _, u, _, _, p, h = pr
    return [q[1], q[1] * u + p, q[2] * u, q[3] * u, h * u]


def flux_r(q, pr):
    _, _, v, _, p, h = pr
    return [q[2], q[1] * v, q[2] * v + p, q[3] * v, h * v]


def flux_t(q, pr):
    _, _, _, w, p, h = pr
    return [q[3], q[1] * w, q[2] * w, q[3] * w + p, h * w]


def pull(q, pr, a, b, c):
    inv, u, v, w, _, h = pr
    ub = a[1] * q[1] + a[2] * q[2] + a[3] * q[3] + a[4] * h
    vb = b[1] * q[1] + b[2] * q[2] + b[3] * q[3] + b[4] * h
    wb = c[1] * q[1] + c[2] * q[2] + c[3] * q[3] + c[4] * h
    hb = a[4] * u + b[4] * v + c[4] * w
    pb = a[1] + b[2] + c[3] + hb
    s = (-0.5 * GAM) * pb
    ub = (ub + s * q[1]) * inv
    vb = (vb + s * q[2]) * inv
    wb = (wb + s * q[3]) * inv
    o1 = a[0] + (a[1] + s) * u + b[1] * v + c[1] * w + ub
    o2 = b[0] + a[2] * u + (b[2] + s) * v + c[2] * w + vb
    o3 = c[0] + a[3] * u + b[3] * v + (c[3] + s) * w + wb
    o4 = hb + GAM * pb
    o0 = -(ub * u + vb * v + wb * w)
    return [o0, o1, o2, o3, o4]


def pull_rt(q, pr, b, c):
    inv, u, v, w, _, h = pr
    hb = b[4] * v + c[4] * w
    pb = b[2] + c[3] + hb
    s = (-0.5 * GAM) * pb
    ub = s * u
    vb = (b[1] * q[1] + b[2] * q[2] + b[3] * q[3] + b[4] * h + s * q[2]) * inv
    wb = (c[1] * q[1] + c[2] * q[2] + c[3] * q[3] + c[4] * h + s * q[3]) * inv
    o1 = s * u + b[1] * v + c[1] * w + ub
    o2 = b[0] + (b[2] + s) * v + c[2] * w + vb
    o3 = c[0] + b[3] * v + (c[3] + s) * w + wb
    o4 = hb + GAM * pb
    o0 = -(ub * u + vb * v + wb * w)
    return [o0, o1, o2, o3, o4]


def iota(shape, dim):
    return lax.broadcasted_iota(jnp.int32, shape, dim)


def metric_tile(met):
    row = iota((NR, NT), 0)
    tile = jnp.zeros((NR, NT), F32)
    for r in range(NR):
        tile = jnp.where(row == r, met[r], tile)
    return tile


def parity(axis):
    return lax.axis_index(axis) % 2


def is_even(axis):
    return jnp.full((NR, NT), parity(axis), jnp.int32) == 0


def split(x):
    hi = x.astype(BF16)
    return hi, (x - hi.astype(F32)).astype(BF16)


def band(coef):
    offset = iota((NT, NT), 0) - iota((NT, NT), 1) + W
    mat = jnp.zeros((NT, NT), F32)
    for j in range(TAPS):
        mat = jnp.where(offset == j, coef[j], mat)
    return mat


def t_own(hi, lo, coef, out):
    bhi, blo = split(band(coef))
    mat = jnp.concatenate([bhi, bhi, blo], axis=0)
    step = 8
    for g in range(NX // step):
        h = hi[pl.ds(g * step, step)].reshape(step * C * NR, NT)
        l = lo[pl.ds(g * step, step)].reshape(step * C * NR, NT)
        total = jnp.dot(jnp.concatenate([h, l, h], axis=1), mat, preferred_element_type=F32)
        out[pl.ds(g * step, step)] = total.reshape(step, C, NR, NT)


def t_pack_coefs(coef):
    lane = iota((NR, NT), 1) % 8
    masks = {}
    for j in range(W):
        masks[j] = jnp.where((lane >= 4) & (lane < 8 - j), coef[j], 0.0)
    for j in range(W + 1, TAPS):
        masks[j] = jnp.where((lane >= 8 - j) & (lane < 4), coef[j], 0.0)
    return masks


def t_halo_packed(rims, masks):
    total = None
    for j, m in masks.items():
        term = m * pltpu.roll(rims, (4 - j) % NT, 1)
        total = term if total is None else total + term
    return total


def t_unpack(packed, k):
    lane = iota((NR, NT), 1)
    moved = pltpu.roll(packed, 124 - 8 * k, 1)
    return jnp.where((lane < 4) | (lane >= 124), moved, 0.0)


def t_pack_one(ref, at, field, k):
    moved = pltpu.roll(field, (8 * k + 4) % NT, 1)
    ref[at] = jnp.where(lane_block() == k, moved, ref[at])


def lane_block():
    return lax.shift_right_logical(iota((NR, NT), 1), 3)


def t_pack_into(ref, base, fields, xx, k):
    for c in range(C):
        t_pack_one(ref, base + 2 * c + xx, fields[c], k)


def r_pack(first, second, even):
    sub = iota((8, NT), 0)
    low = jnp.where(sub < 4, first[:8], pltpu.roll(second[:8], 4, 0))
    high = jnp.where(sub < 4, pltpu.roll(first[8:], 4, 0), second[8:])
    ev = even[:8]
    return jnp.where(ev, high, low), jnp.where(ev, low, high)


def r_coefs(coef):
    sub = iota((8, NT), 0)
    low = [jnp.where(sub < 4 - j, coef[j], 0.0) for j in range(W)]
    high = {j: jnp.where(sub >= 12 - j, coef[j], 0.0) for j in range(W + 1, TAPS)}
    return low, high


def r_halo(low, high, xlo, xhi, coefs):
    lo_c, hi_c = coefs
    top = None
    for j in range(W):
        shift = (8 - (4 * xlo + j)) % 8
        term = lo_c[j] * (pltpu.roll(low, shift, 0) if shift else low)
        top = term if top is None else top + term
    bottom = None
    for j in range(W + 1, TAPS):
        shift = (12 - j - 4 * xhi) % 8
        term = hi_c[j] * (pltpu.roll(high, shift, 0) if shift else high)
        bottom = term if bottom is None else bottom + term
    return jnp.concatenate([top, bottom], axis=0)


def x_taps(read, x, coef):
    total = None
    for j in range(TAPS):
        at = x + j - W
        if isinstance(x, int) and not 0 <= at < NX:
            continue
        term = coef[j] * read(at)
        total = term if total is None else total + term
    return total


def x_halo(planes, i, low, coef):
    total = None
    for j in range(TAPS):
        at = i + j if low else i + j - 8
        if not 0 <= at < W:
            continue
        term = coef[j] * planes[at]
        total = term if total is None else total + term
    return total


def over_planes(body):
    for x in range(W):
        body(x)

    def step(x, carry):
        body(x)
        return carry

    lax.fori_loop(W, NX - W, step, 0)
    for x in range(NX - W, NX):
        body(x)


def loop(lo, hi, body, unroll=1):
    def step(k, carry):
        body(k)
        return carry

    lax.fori_loop(lo, hi, step, 0, unroll=unroll)


def rim_starts():
    even = parity("gx") == 0
    return jnp.where(even, NX - W, 0), jnp.where(even, 0, NX - W)


def first(cf, state_hbm, seed_hbm, state, seed, prim, xe, xo, sems):
    moves = [
        pltpu.make_async_copy(seed_hbm, seed, sems.at[0]),
        pltpu.make_async_copy(state_hbm, state, sems.at[1]),
    ]
    for move in moves:
        move.start()
    fc = [-cf[TAPS - 1 - j] for j in range(TAPS)]
    moves[0].wait()
    for side, base in enumerate((0, NX - W)):
        for i in range(W):
            for c in range(C):
                prim[side, c, i] = seed[c, base + i] + x_taps(lambda at: seed[c, at], base + i, fc)
    starts = rim_starts()
    even = parity("gx") == 0
    sides = jnp.where(even, 1, 0), jnp.where(even, 0, 1)
    moves[1].wait()
    for start, side, out in zip(starts, sides, (xe, xo)):
        for i in range(W):
            q = [state[c, start + i] for c in range(C)]
            f = flux_x(q, prims(q))
            for c in range(C):
                out[c, i] = f[c]
                out[C + c, i] = seed[c, start + i]
                out[2 * C + c, i] = prim[side, c, i]


def second(cf, met, state, seed, prim, plam, re, ro, th):
    fc = [-cf[TAPS - 1 - j] for j in range(TAPS)]
    mt = metric_tile(met)
    even = is_even("row")
    th[...] = jnp.zeros(th.shape, F32)
    for side, base in enumerate((0, NX - W)):
        for i in range(W):
            for c in range(C):
                plam[c, base + i] = prim[side, c, i]

    def plane(x):
        for c in range(C):
            plam[c, x] = seed[c, x] + x_taps(lambda at: seed[c, at], x, fc)

    loop(W, NX - W, plane, 2)

    def pair(k):
        keep = []
        for xx in range(2):
            q = [state[c, 2 * k + xx] for c in range(C)]
            pr = prims(q)
            keep.append(flux_r(q, pr))
            t_pack_into(th, 0, flux_t(q, pr), xx, k)
            t_pack_into(th, 2 * C, [mt * plam[c, 2 * k + xx] for c in range(C)], xx, k)
        for c in range(C):
            re[c, k], ro[c, k] = r_pack(keep[0][c], keep[1][c], even)
            at = NX // 2 + k
            re[c, at], ro[c, at] = r_pack(plam[c, 2 * k], plam[c, 2 * k + 1], even)

    loop(0, NX // 2, pair, 2)
    for n, k in enumerate(RIM_PAIRS):
        for c in range(C):
            at = NX + n
            re[c, at], ro[c, at] = r_pack(seed[c, 2 * k], seed[c, 2 * k + 1], even)
            for xx in range(2):
                t_pack_one(th, 4 * C + 2 * (c // 4) + xx, seed[c, 2 * k + xx], n + 4 * (c % 4))


def own(cx, cr, ct, met, state, psec, fx, fr, hi, lo, tt):
    mt = metric_tile(met)
    zero = jnp.zeros((8, NT), F32)

    def fill(x):
        q = [state[c, x] for c in range(C)]
        pr = prims(q)
        f, g, h = flux_x(q, pr), flux_r(q, pr), flux_t(q, pr)
        for c in range(C):
            fx[c, x] = f[c]
            fr[c, x, 0:8] = zero
            fr[c, x, 8:24] = g[c]
            fr[c, x, 24:32] = zero
            hi[x, c], lo[x, c] = split(h[c])

    loop(0, NX, fill)
    t_own(hi, lo, [-DT * ct[j] for j in range(TAPS)], tt)
    xc = [-DT * cx[j] for j in range(TAPS)]
    rc = [-DT * cr[j] for j in range(TAPS)]

    def plane(x):
        for c in range(C):
            acc = state[c, x] + mt * tt[x, c]
            acc += x_taps(lambda at: fx[c, at], x, xc)
            for j in range(TAPS):
                acc += rc[j] * fr[c, x, 4 + j : 20 + j]
            psec[c, x] = acc

    over_planes(plane)


def join(cx, cr, ct, cf, met, seed, psec, plam, xe, xo, re, ro, th, sec, lam, lamh, xe2, xo2):
    mt = metric_tile(met)
    evx, evr = is_even("gx"), is_even("row")
    fc = [-cf[TAPS - 1 - j] for j in range(TAPS)]
    xc = [-DT * cx[j] for j in range(TAPS)]
    place = jnp.full((NR, NT), lax.axis_index("gx"), jnp.int32)
    has = place > 0, place < lax.axis_size("gx") - 1
    for side, base in enumerate((0, NX - W)):
        low = side == 0
        near_, far = (xo, xe) if low else (xe, xo)

        def halo(c):
            return [jnp.where(evx, near_[c, i], far[c, i]) for i in range(W)]

        for c in range(C):
            flux, seeds, share = halo(c), halo(C + c), halo(2 * C + c)
            mine = [seed[c, base + i] for i in range(W)]
            for i in range(W):
                sec[c, base + i] = psec[c, base + i] + x_halo(flux, i, low, xc)
                lam[c, base + i] = plam[c, base + i] + x_halo(seeds, i, low, fc)
                value = share[i] + x_halo(mine, i, not low, fc)
                lamh[side, c, i] = jnp.where(has[side], value, 0.0)
    rc = r_coefs([-DT * cr[j] for j in range(TAPS)])
    tc = t_pack_coefs([-DT * ct[j] for j in range(TAPS)])
    packed = [[mt * t_halo_packed(th[2 * c + xx], tc) for xx in range(2)] for c in range(C)]
    ev8 = evr[:8]

    def pair(k, s_ref, inside):
        for c in range(C):
            a, b = re[c, k], ro[c, k]
            low, high = jnp.where(ev8, b, a), jnp.where(ev8, a, b)
            for xx in range(2):
                x = 2 * k + xx
                share = r_halo(low, high, xx, xx, rc) + t_unpack(packed[c][xx], k)
                sec[c, x] = s_ref[c, x] + share
                if inside:
                    lam[c, x] = plam[c, x]

    def send():
        starts = rim_starts()
        even = parity("gx") == 0
        corners = NX + jnp.where(even, 2, 0), NX + jnp.where(even, 0, 2)
        for start, corner, out in zip(starts, corners, (xe2, xo2)):
            for c in range(C):
                for i in range(W):
                    out[W * c + i] = sec[c, start + i]
                for eo, src in enumerate((re, ro)):
                    for p in range(2):
                        out[W * C + 2 * c + eo, 8 * p : 8 * p + 8] = src[c, corner + p]
            for t in range(4):
                out[(W + 2) * C + t] = th[4 * C + t]

    loop(0, 2, functools.partial(pair, s_ref=sec, inside=False))
    loop(14, 16, functools.partial(pair, s_ref=sec, inside=False))
    send()
    loop(2, 14, functools.partial(pair, s_ref=psec, inside=True))


def finish(
    cx, cr, ct, cf, met, state, sec, lam, lamh, re, ro, th,
    new, adj, nrim, arim, lr, hi, lo, tt, nb, ab, sems,
):
    mt = metric_tile(met)
    evr = is_even("row")
    ev8 = evr[:8]
    rx = [-DT * cx[TAPS - 1 - j] for j in range(TAPS)]
    rr = [-DT * cr[TAPS - 1 - j] for j in range(TAPS)]
    rt = [-DT * ct[TAPS - 1 - j] for j in range(TAPS)]
    tc = t_pack_coefs(rt)
    packed = [[t_halo_packed(th[2 * C + 2 * c + xx], tc) for xx in range(2)] for c in range(C)]

    def fill(k):
        for c in range(C):
            at = NX // 2 + k
            a, b = re[c, at], ro[c, at]
            low, high = jnp.where(ev8, b, a), jnp.where(ev8, a, b)
            for xx in range(2):
                x = 2 * k + xx
                value = lam[c, x]
                lr[c, x, 0:8] = low if xx else pltpu.roll(low, 4, 0)
                lr[c, x, 8:24] = value
                lr[c, x, 24:32] = pltpu.roll(high, 4, 0) if xx else high
                hi[x, c], lo[x, c] = split(mt * value)

    loop(0, NX // 2, fill)
    t_own(hi, lo, rt, tt)

    def add(k):
        for c in range(C):
            for xx in range(2):
                tt[2 * k + xx, c] += t_unpack(packed[c][xx], k)

    loop(0, NX // 2, add)
    fcs = [cf[j] for j in range(TAPS)]

    def plane(x):
        q = [state[c, x] for c in range(C)]
        pr = prims(q)
        rim = isinstance(x, int)
        side, at = (0, x) if rim and x < W else (1, x - NX + W)
        a, b, g = [], [], []
        for c in range(C):
            acc = x_taps(lambda at: lam[c, at], x, rx)
            if rim:
                acc += x_halo([lamh[side, c, h] for h in range(W)], at, side == 0, rx)
            a.append(acc)
            acc = None
            for j in range(TAPS):
                term = rr[j] * lr[c, x, 4 + j : 20 + j]
                acc = term if acc is None else acc + term
            b.append(acc)
            g.append(tt[x, c])
        out = pull(q, pr, a, b, g)
        for c in range(C):
            av = lam[c, x] + out[c]
            nv = sec[c, x] - x_taps(lambda at: sec[c, at], x, fcs)
            if rim:
                arim[side, c, at], nrim[side, c, at] = av, nv
            else:
                ab[c, x - W], nb[c, x - W] = av, nv

    lax.fori_loop(W, NX - W, lambda x, carry: (plane(x), carry)[1], 0)
    inside = pl.ds(W, NX - 2 * W)
    moves = [
        pltpu.make_async_copy(ab, adj.at[:, inside], sems.at[0]),
        pltpu.make_async_copy(nb, new.at[:, inside], sems.at[1]),
    ]
    for move in moves:
        move.start()
    for x in (*range(W), *range(NX - W, NX)):
        plane(x)
    for move in moves:
        move.wait()


def edges(cr, ct, cf, met, state, xe2, xo2, nrim, arim, nin, ain, nout, aout, nb, ab, sems):
    mt = metric_tile(met)
    evx, evr = is_even("gx"), is_even("row")
    ev8 = evr[:8]
    sub = iota((8, NT), 0)
    fc = [-cf[TAPS - 1 - j] for j in range(TAPS)]
    fcs = [cf[j] for j in range(TAPS)]
    rc = r_coefs([-DT * cr[TAPS - 1 - j] for j in range(TAPS)])
    tc = t_pack_coefs([-DT * ct[TAPS - 1 - j] for j in range(TAPS)])
    starts = (0, NX - W)
    moves = []

    def put(buf, dst, side, slot):
        move = pltpu.make_async_copy(
            buf.at[side], dst.at[:, pl.ds(starts[side], W)], sems.at[slot + side]
        )
        move.start()
        moves.append(move)

    for side, at in enumerate(starts):
        low = side == 0
        mine, other = (xo2, xe2) if low else (xe2, xo2)

        def got(n):
            return jnp.where(evx, mine[n], other[n])

        for c in range(C):
            planes = [got(W * c + i) for i in range(W)]
            for i in range(W):
                nb[side, c, i] = nrim[side, c, i] - x_halo(planes, i, low, fcs)
        put(nb, nout, side, 0)
        b, g = [], []
        for c in range(C):
            one, two = got(W * C + 2 * c), got(W * C + 2 * c + 1)
            rows, lanes = [], []
            for p in range(2):
                e, o = one[8 * p : 8 * p + 8], two[8 * p : 8 * p + 8]
                lt, ht = jnp.where(ev8, o, e), jnp.where(ev8, e, o)
                rows.append(jnp.where(sub < 4, lt, pltpu.roll(ht, 4, 0)))
                rows.append(jnp.where(sub < 4, pltpu.roll(lt, 4, 0), ht))
                block = (2 if low else 0) + p + 4 * (c % 4)
                for xx in range(2):
                    tile = got((W + 2) * C + 2 * (c // 4) + xx)
                    lanes.append(pltpu.roll(tile, NT - 8 * block, 1) if block else tile)
            bc, gc = [], []
            for i in range(W):
                row = x_halo(rows, i, low, fc)
                bc.append(r_halo(row, row, 0, 1, rc))
                lane = mt * x_halo(lanes, i, low, fc)
                gc.append(t_unpack(t_halo_packed(lane, tc), 0))
            b.append(bc)
            g.append(gc)
        for i in range(W):
            q = [state[c, at + i] for c in range(C)]
            out = pull_rt(q, prims(q), [b[c][i] for c in range(C)], [g[c][i] for c in range(C)])
            for c in range(C):
                ab[side, c, i] = arim[side, c, i] + out[c]
        put(ab, aout, side, 2)
    for move in moves:
        move.wait()


def near(value):
    return pltpu.with_memory_space_constraint(value, pltpu.VMEM)


LIMIT = pltpu.CompilerParams(vmem_limit_bytes=24 << 20)
FULL = (C, NX, NR, NT)
XPAY = (3 * C, W, NR, NT)
XPAY2 = ((W + 2) * C + 4, NR, NT)
RPAY = (C, NX + 4, 8, NT)
TPAY = (4 * C + 4, NR, NT)
RIM = (2, C, W, NR, NT)
RIM_PAIRS = (0, 1, NX // 2 - 2, NX // 2 - 1)


def call(kernel, smem, vmem, outs, scratch=()):
    run = pl.pallas_call(
        kernel,
        in_specs=[SM] * len(smem) + [VM] * len(vmem),
        out_specs=[VM] * len(outs),
        out_shape=[pltpu.VMEM(s, F32) for s in outs],
        scratch_shapes=list(scratch),
        compiler_params=LIMIT,
    )
    return run(*smem, *[near(v) for v in vmem])


def swap(value, axis, odd):
    count = lax.axis_size(axis)
    pairs = []
    for i in range(odd, count - 1, 2):
        pairs += [(i, i + 1), (i + 1, i)]
    return lax.ppermute(value, axis, pairs)


def across(value):
    return lax.ppermute(value, "th", [(0, 1), (1, 0)])


SPLIT = [pltpu.VMEM((NX, C, NR, NT), BF16), pltpu.VMEM((NX, C, NR, NT), BF16), pltpu.VMEM((NX, C, NR, NT), F32)]
WIDE_R = pltpu.VMEM((C, NX, 32, NT), F32)


def shards(state, seed, cx, cr, ct, cf, met):
    shapes = [FULL, FULL, RIM, XPAY, XPAY]
    state, seed, prim, xe, xo = pl.pallas_call(
        first,
        in_specs=[SM] + [pl.BlockSpec(memory_space=pltpu.HBM)] * 2,
        out_specs=[VM] * len(shapes),
        out_shape=[pltpu.VMEM(s, F32) for s in shapes],
        scratch_shapes=[pltpu.SemaphoreType.DMA((2,))],
        name="first",
        compiler_params=LIMIT,
    )(cf, *[pltpu.with_memory_space_constraint(v, pltpu.HBM) for v in (state, seed)])
    xe = swap(xe, "gx", 0)
    xo = swap(xo, "gx", 1)
    plam, re, ro, th = call(second, [cf, met], [state, seed, prim], [FULL, RPAY, RPAY, TPAY])
    th = across(th)
    re = swap(re, "row", 0)
    ro = swap(ro, "row", 1)
    (psec,) = call(
        own, [cx, cr, ct, met], [state], [FULL], [pltpu.VMEM(FULL, F32), WIDE_R] + SPLIT
    )
    sec, lam, lamh, xe2, xo2 = call(
        join,
        [cx, cr, ct, cf, met],
        [seed, psec, plam, xe, xo, re, ro, th],
        [FULL, FULL, RIM, XPAY2, XPAY2],
    )
    xe2 = swap(xe2, "gx", 0)
    xo2 = swap(xo2, "gx", 1)
    inner = pltpu.VMEM((C, NX - 2 * W, NR, NT), F32)
    whole = jax.ShapeDtypeStruct(FULL, F32)
    new, adj, nrim, arim = pl.pallas_call(
        finish,
        in_specs=[SM] * 5 + [VM] * 7,
        out_specs=[ANY, ANY, VM, VM],
        out_shape=[whole, whole, pltpu.VMEM(RIM, F32), pltpu.VMEM(RIM, F32)],
        scratch_shapes=[WIDE_R] + SPLIT + [inner, inner, pltpu.SemaphoreType.DMA((2,))],
        name="finish",
        compiler_params=LIMIT,
    )(cx, cr, ct, cf, met, *map(near, (state, sec, lam, lamh, re, ro, th)))
    return pl.pallas_call(
        edges,
        in_specs=[SM] * 4 + [VM] * 5 + [ANY] * 2,
        out_specs=[ANY, ANY],
        out_shape=[whole, whole],
        scratch_shapes=[pltpu.VMEM(RIM, F32), pltpu.VMEM(RIM, F32), pltpu.SemaphoreType.DMA((4,))],
        input_output_aliases={9: 0, 10: 1},
        name="edges",
        compiler_params=LIMIT,
    )(cr, ct, cf, met, *map(near, (state, xe2, xo2, nrim, arim)), new, adj)


def solution(mesh):
    whole = P(None, "gx", "row", "th")

    return jax.shard_map(
        shards,
        mesh=mesh,
        in_specs=(whole, whole, P(), P(), P(), P(), P("row")),
        out_specs=(whole, whole),
        check_vma=False,
    )
```

```python
import jax
import jax.numpy as jnp
from jax import lax
from jax.experimental import pallas as pl
from jax.experimental.pallas import tpu as pltpu
from jax.sharding import PartitionSpec as P


DT = 0.1
GAM = 0.4
W = 4
TAPS = 9
C = 5
NX, NR, NT = 32, 16, 128
F32 = jnp.float32
BF16 = jnp.bfloat16
VM = pl.BlockSpec(memory_space=pltpu.VMEM)
SM = pl.BlockSpec(memory_space=pltpu.SMEM)
ANY = pl.BlockSpec(memory_space=pl.ANY)


def prims(q):
    inv = 1.0 / q[0]
    u, v, w = q[1] * inv, q[2] * inv, q[3] * inv
    p = GAM * (q[4] - 0.5 * (q[1] * u + q[2] * v + q[3] * w))
    return inv, u, v, w, p, q[4] + p


def flux_x(q, pr):
    _, u, _, _, p, h = pr
    return [q[1], q[1] * u + p, q[2] * u, q[3] * u, h * u]


def flux_r(q, pr):
    _, _, v, _, p, h = pr
    return [q[2], q[1] * v, q[2] * v + p, q[3] * v, h * v]


def flux_t(q, pr):
    _, _, _, w, p, h = pr
    return [q[3], q[1] * w, q[2] * w, q[3] * w + p, h * w]


def pull(q, pr, a, b, c):
    inv, u, v, w, _, h = pr
    ub = a[1] * q[1] + a[2] * q[2] + a[3] * q[3] + a[4] * h
    vb = b[1] * q[1] + b[2] * q[2] + b[3] * q[3] + b[4] * h
    wb = c[1] * q[1] + c[2] * q[2] + c[3] * q[3] + c[4] * h
    hb = a[4] * u + b[4] * v + c[4] * w
    pb = a[1] + b[2] + c[3] + hb
    s = (-0.5 * GAM) * pb
    ub = (ub + s * q[1]) * inv
    vb = (vb + s * q[2]) * inv
    wb = (wb + s * q[3]) * inv
    o1 = a[0] + (a[1] + s) * u + b[1] * v + c[1] * w + ub
    o2 = b[0] + a[2] * u + (b[2] + s) * v + c[2] * w + vb
    o3 = c[0] + a[3] * u + b[3] * v + (c[3] + s) * w + wb
    o4 = hb + GAM * pb
    o0 = -(ub * u + vb * v + wb * w)
    return [o0, o1, o2, o3, o4]


def pull_rt(q, pr, b, c):
    inv, u, v, w, _, h = pr
    hb = b[4] * v + c[4] * w
    pb = b[2] + c[3] + hb
    s = (-0.5 * GAM) * pb
    ub = s * u
    vb = (b[1] * q[1] + b[2] * q[2] + b[3] * q[3] + b[4] * h + s * q[2]) * inv
    wb = (c[1] * q[1] + c[2] * q[2] + c[3] * q[3] + c[4] * h + s * q[3]) * inv
    o1 = s * u + b[1] * v + c[1] * w + ub
    o2 = b[0] + (b[2] + s) * v + c[2] * w + vb
    o3 = c[0] + b[3] * v + (c[3] + s) * w + wb
    o4 = hb + GAM * pb
    o0 = -(ub * u + vb * v + wb * w)
    return [o0, o1, o2, o3, o4]


def iota(shape, dim):
    return lax.broadcasted_iota(jnp.int32, shape, dim)


def metric_tile(met):
    row = iota((NR, NT), 0)
    tile = jnp.zeros((NR, NT), F32)
    for r in range(NR):
        tile = jnp.where(row == r, met[r], tile)
    return tile


def parity(axis):
    return lax.axis_index(axis) % 2


def is_even(axis):
    return jnp.full((NR, NT), parity(axis), jnp.int32) == 0


def split(x):
    hi = x.astype(BF16)
    return hi, (x - hi.astype(F32)).astype(BF16)


def band(coef):
    offset = iota((NT, NT), 0) - iota((NT, NT), 1) + W
    mat = jnp.zeros((NT, NT), F32)
    for j in range(TAPS):
        mat = jnp.where(offset == j, coef[j], mat)
    return mat


def t_own(hi, lo, coef, out):
    bhi, blo = split(band(coef))
    mat = jnp.concatenate([bhi, bhi, blo], axis=0)
    step = 8
    for g in range(NX // step):
        h = hi[pl.ds(g * step, step)].reshape(step * C * NR, NT)
        l = lo[pl.ds(g * step, step)].reshape(step * C * NR, NT)
        total = jnp.dot(jnp.concatenate([h, l, h], axis=1), mat, preferred_element_type=F32)
        out[pl.ds(g * step, step)] = total.reshape(step, C, NR, NT)


def t_pack_coefs(coef):
    lane = iota((NR, NT), 1) % 8
    masks = {}
    for j in range(W):
        masks[j] = jnp.where((lane >= 4) & (lane < 8 - j), coef[j], 0.0)
    for j in range(W + 1, TAPS):
        masks[j] = jnp.where((lane >= 8 - j) & (lane < 4), coef[j], 0.0)
    return masks


def t_halo_packed(rims, masks):
    total = None
    for j, m in masks.items():
        term = m * pltpu.roll(rims, (4 - j) % NT, 1)
        total = term if total is None else total + term
    return total


def t_unpack(packed, k):
    lane = iota((NR, NT), 1)
    moved = pltpu.roll(packed, 124 - 8 * k, 1)
    return jnp.where((lane < 4) | (lane >= 124), moved, 0.0)


def t_pack_one(ref, at, field, k):
    moved = pltpu.roll(field, (8 * k + 4) % NT, 1)
    ref[at] = jnp.where(lane_block() == k, moved, ref[at])


def lane_block():
    return lax.shift_right_logical(iota((NR, NT), 1), 3)


def t_pack_into(ref, base, fields, xx, k):
    for c in range(C):
        t_pack_one(ref, base + 2 * c + xx, fields[c], k)


def r_pack(first, second, even):
    sub = iota((8, NT), 0)
    low = jnp.where(sub < 4, first[:8], pltpu.roll(second[:8], 4, 0))
    high = jnp.where(sub < 4, pltpu.roll(first[8:], 4, 0), second[8:])
    ev = even[:8]
    return jnp.where(ev, high, low), jnp.where(ev, low, high)


def r_coefs(coef):
    sub = iota((8, NT), 0)
    low = [jnp.where(sub < 4 - j, coef[j], 0.0) for j in range(W)]
    high = {j: jnp.where(sub >= 12 - j, coef[j], 0.0) for j in range(W + 1, TAPS)}
    return low, high


def r_halo(low, high, xlo, xhi, coefs):
    lo_c, hi_c = coefs
    top = None
    for j in range(W):
        shift = (8 - (4 * xlo + j)) % 8
        term = lo_c[j] * (pltpu.roll(low, shift, 0) if shift else low)
        top = term if top is None else top + term
    bottom = None
    for j in range(W + 1, TAPS):
        shift = (12 - j - 4 * xhi) % 8
        term = hi_c[j] * (pltpu.roll(high, shift, 0) if shift else high)
        bottom = term if bottom is None else bottom + term
    return jnp.concatenate([top, bottom], axis=0)


def x_taps(read, x, coef):
    total = None
    for j in range(TAPS):
        at = x + j - W
        if isinstance(x, int) and not 0 <= at < NX:
            continue
        term = coef[j] * read(at)
        total = term if total is None else total + term
    return total


def x_halo(planes, i, low, coef):
    total = None
    for j in range(TAPS):
        at = i + j if low else i + j - 8
        if not 0 <= at < W:
            continue
        term = coef[j] * planes[at]
        total = term if total is None else total + term
    return total


def over_planes(body):
    for x in range(W):
        body(x)

    def step(x, carry):
        body(x)
        return carry

    lax.fori_loop(W, NX - W, step, 0)
    for x in range(NX - W, NX):
        body(x)


def loop(lo, hi, body, unroll=1):
    def step(k, carry):
        body(k)
        return carry

    lax.fori_loop(lo, hi, step, 0, unroll=unroll)


def rim_starts():
    even = parity("gx") == 0
    return jnp.where(even, NX - W, 0), jnp.where(even, 0, NX - W)


def first(cf_hbm, state_hbm, seed_hbm, state, seed, prim, xe, xo, cf, sems):
    moves = [
        pltpu.make_async_copy(seed_hbm, seed, sems.at[0]),
        pltpu.make_async_copy(state_hbm, state, sems.at[1]),
        pltpu.make_async_copy(cf_hbm, cf, sems.at[2]),
    ]
    for move in moves:
        move.start()
    moves[2].wait()
    fc = [-cf[TAPS - 1 - j] for j in range(TAPS)]
    moves[0].wait()
    for side, base in enumerate((0, NX - W)):
        for i in range(W):
            for c in range(C):
                prim[side, c, i] = seed[c, base + i] + x_taps(lambda at: seed[c, at], base + i, fc)
    starts = rim_starts()
    even = parity("gx") == 0
    sides = jnp.where(even, 1, 0), jnp.where(even, 0, 1)
    moves[1].wait()
    for start, side, out in zip(starts, sides, (xe, xo)):
        for i in range(W):
            q = [state[c, start + i] for c in range(C)]
            f = flux_x(q, prims(q))
            for c in range(C):
                out[c, i] = f[c]
                out[C + c, i] = seed[c, start + i]
                out[2 * C + c, i] = prim[side, c, i]


def second(cf, met, state, seed, prim, plam, re, ro, th):
    fc = [-cf[TAPS - 1 - j] for j in range(TAPS)]
    mt = metric_tile(met)
    even = is_even("row")
    th[...] = jnp.zeros(th.shape, F32)
    for side, base in enumerate((0, NX - W)):
        for i in range(W):
            for c in range(C):
                plam[c, base + i] = prim[side, c, i]

    def plane(x):
        for c in range(C):
            plam[c, x] = seed[c, x] + x_taps(lambda at: seed[c, at], x, fc)

    loop(W, NX - W, plane, 2)

    def pair(k):
        keep = []
        for xx in range(2):
            q = [state[c, 2 * k + xx] for c in range(C)]
            pr = prims(q)
            keep.append(flux_r(q, pr))
            t_pack_into(th, 0, flux_t(q, pr), xx, k)
            t_pack_into(th, 2 * C, [mt * plam[c, 2 * k + xx] for c in range(C)], xx, k)
        for c in range(C):
            re[c, k], ro[c, k] = r_pack(keep[0][c], keep[1][c], even)
            at = NX // 2 + k
            re[c, at], ro[c, at] = r_pack(plam[c, 2 * k], plam[c, 2 * k + 1], even)

    loop(0, NX // 2, pair, 2)
    for n, k in enumerate(RIM_PAIRS):
        for c in range(C):
            at = NX + n
            re[c, at], ro[c, at] = r_pack(seed[c, 2 * k], seed[c, 2 * k + 1], even)
            for xx in range(2):
                t_pack_one(th, 4 * C + 2 * (n // 2) + xx, seed[c, 2 * k + xx], n % 2 + 2 * c)


def own(cx, cr, ct, met, state, psec, fx, fr, hi, lo, tt):
    mt = metric_tile(met)
    zero = jnp.zeros((8, NT), F32)

    def fill(x):
        q = [state[c, x] for c in range(C)]
        pr = prims(q)
        f, g, h = flux_x(q, pr), flux_r(q, pr), flux_t(q, pr)
        for c in range(C):
            fx[c, x] = f[c]
            fr[c, x, 0:8] = zero
            fr[c, x, 8:24] = g[c]
            fr[c, x, 24:32] = zero
            hi[x, c], lo[x, c] = split(h[c])

    loop(0, NX, fill)
    t_own(hi, lo, [-DT * ct[j] for j in range(TAPS)], tt)
    xc = [-DT * cx[j] for j in range(TAPS)]
    rc = [-DT * cr[j] for j in range(TAPS)]

    def plane(x):
        for c in range(C):
            acc = state[c, x] + mt * tt[x, c]
            acc += x_taps(lambda at: fx[c, at], x, xc)
            for j in range(TAPS):
                acc += rc[j] * fr[c, x, 4 + j : 20 + j]
            psec[c, x] = acc

    over_planes(plane)


def join(cx, cr, ct, cf, met, seed, psec, plam, xe, xo, re, ro, th, srim, lrim, lamh, xe2, xo2):
    mt = metric_tile(met)
    evx, evr = is_even("gx"), is_even("row")
    fc = [-cf[TAPS - 1 - j] for j in range(TAPS)]
    xc = [-DT * cx[j] for j in range(TAPS)]
    place = jnp.full((NR, NT), lax.axis_index("gx"), jnp.int32)
    has = place > 0, place < lax.axis_size("gx") - 1
    for side, base in enumerate((0, NX - W)):
        low = side == 0
        near_, far = (xo, xe) if low else (xe, xo)

        def halo(c):
            return [jnp.where(evx, near_[c, i], far[c, i]) for i in range(W)]

        for c in range(C):
            flux, seeds, share = halo(c), halo(C + c), halo(2 * C + c)
            mine = [seed[c, base + i] for i in range(W)]
            for i in range(W):
                srim[side, c, i] = psec[c, base + i] + x_halo(flux, i, low, xc)
                lrim[side, c, i] = plam[c, base + i] + x_halo(seeds, i, low, fc)
                value = share[i] + x_halo(mine, i, not low, fc)
                lamh[side, c, i] = jnp.where(has[side], value, 0.0)
    share = rt_share(cr, ct, mt, evr[:8], re, ro, th)
    for n, k in enumerate(RIM_PAIRS):
        for c in range(C):
            for xx, value in enumerate(share(c, k)):
                srim[n // 2, c, 2 * (n % 2) + xx] += value
    even = parity("gx") == 0
    sides = jnp.where(even, 1, 0), jnp.where(even, 0, 1)
    for side, out in zip(sides, (xe2, xo2)):
        for c in range(C):
            for i in range(W):
                out[W * c + i] = srim[side, c, i]
            for eo, src in enumerate((re, ro)):
                for p in range(2):
                    out[W * C + 2 * c + eo, 8 * p : 8 * p + 8] = src[c, NX + 2 * side + p]
        for xx in range(2):
            out[(W + 2) * C + xx] = th[4 * C + 2 * side + xx]


def rt_share(cr, ct, mt, ev8, re, ro, th):
    rc = r_coefs([-DT * cr[j] for j in range(TAPS)])
    tc = t_pack_coefs([-DT * ct[j] for j in range(TAPS)])
    packed = [[mt * t_halo_packed(th[2 * c + xx], tc) for xx in range(2)] for c in range(C)]

    def share(c, k):
        a, b = re[c, k], ro[c, k]
        low, high = jnp.where(ev8, b, a), jnp.where(ev8, a, b)
        return [r_halo(low, high, xx, xx, rc) + t_unpack(packed[c][xx], k) for xx in range(2)]

    return share


def finish(
    cx, cr, ct, cf, met, state, psec, plam, srim, lrim, lamh, re, ro, th,
    new, adj, nrim, arim, sec, lam, pk, lr, hi, lo, tt, nb, ab, sems,
):
    mt = metric_tile(met)
    evr = is_even("row")
    ev8 = evr[:8]
    rx = [-DT * cx[TAPS - 1 - j] for j in range(TAPS)]
    rr = [-DT * cr[TAPS - 1 - j] for j in range(TAPS)]
    rt = [-DT * ct[TAPS - 1 - j] for j in range(TAPS)]
    tc = t_pack_coefs(rt)
    for c in range(C):
        for xx in range(2):
            pk[xx, c] = t_halo_packed(th[2 * C + 2 * c + xx], tc)
        for side, base in enumerate((0, NX - W)):
            for i in range(W):
                sec[c, base + i], lam[c, base + i] = srim[side, c, i], lrim[side, c, i]
    share = rt_share(cr, ct, mt, ev8, re, ro, th)

    def inner(k):
        for c in range(C):
            for xx, value in enumerate(share(c, k)):
                x = 2 * k + xx
                sec[c, x] = psec[c, x] + value
                lam[c, x] = plam[c, x]

    loop(2, 14, inner)

    def fill(k):
        for c in range(C):
            at = NX // 2 + k
            a, b = re[c, at], ro[c, at]
            low, high = jnp.where(ev8, b, a), jnp.where(ev8, a, b)
            for xx in range(2):
                x = 2 * k + xx
                value = lam[c, x]
                lr[c, x, 0:8] = low if xx else pltpu.roll(low, 4, 0)
                lr[c, x, 8:24] = value
                lr[c, x, 24:32] = pltpu.roll(high, 4, 0) if xx else high
                hi[x, c], lo[x, c] = split(mt * value)

    loop(0, NX // 2, fill)
    t_own(hi, lo, rt, tt)

    fcs = [cf[j] for j in range(TAPS)]

    def plane(x):
        q = [state[c, x] for c in range(C)]
        pr = prims(q)
        rim = isinstance(x, int)
        side, at = (0, x) if rim and x < W else (1, x - NX + W)
        a, b, g = [], [], []
        for c in range(C):
            acc = x_taps(lambda at: lam[c, at], x, rx)
            if rim:
                acc += x_halo([lamh[side, c, h] for h in range(W)], at, side == 0, rx)
            a.append(acc)
            acc = None
            for j in range(TAPS):
                term = rr[j] * lr[c, x, 4 + j : 20 + j]
                acc = term if acc is None else acc + term
            b.append(acc)
            g.append(tt[x, c] + t_unpack(pk[x % 2, c], x // 2))
        out = pull(q, pr, a, b, g)
        for c in range(C):
            av = lam[c, x] + out[c]
            nv = sec[c, x] - x_taps(lambda at: sec[c, at], x, fcs)
            if rim:
                arim[side, c, at], nrim[side, c, at] = av, nv
            else:
                ab[c, x - W], nb[c, x - W] = av, nv

    lax.fori_loop(W, NX - W, lambda x, carry: (plane(x), carry)[1], 0)
    inside = pl.ds(W, NX - 2 * W)
    moves = [
        pltpu.make_async_copy(ab, adj.at[:, inside], sems.at[0]),
        pltpu.make_async_copy(nb, new.at[:, inside], sems.at[1]),
    ]
    for move in moves:
        move.start()
    for x in (*range(W), *range(NX - W, NX)):
        plane(x)
    for move in moves:
        move.wait()


def edges(cr, ct, cf, met, state, xe2, xo2, nrim, arim, nin, ain, nout, aout, nb, ab, bs, gs, sems):
    mt = metric_tile(met)
    evx, evr = is_even("gx"), is_even("row")
    ev8 = evr[:8]
    sub = iota((8, NT), 0)
    fc = [-cf[TAPS - 1 - j] for j in range(TAPS)]
    fcs = [cf[j] for j in range(TAPS)]
    rc = r_coefs([-DT * cr[TAPS - 1 - j] for j in range(TAPS)])
    tc = t_pack_coefs([-DT * ct[TAPS - 1 - j] for j in range(TAPS)])
    starts = (0, NX - W)
    moves = []

    def put(buf, dst, side, slot):
        move = pltpu.make_async_copy(
            buf.at[side], dst.at[:, pl.ds(starts[side], W)], sems.at[slot + side]
        )
        move.start()
        moves.append(move)

    for side, at in enumerate(starts):
        low = side == 0
        mine, other = (xo2, xe2) if low else (xe2, xo2)

        def got(n):
            return jnp.where(evx, mine[n], other[n])

        for c in range(C):
            planes = [got(W * c + i) for i in range(W)]
            for i in range(W):
                nb[side, c, i] = nrim[side, c, i] - x_halo(planes, i, low, fcs)
        put(nb, nout, side, 0)
        turned = [t_halo_packed(got((W + 2) * C + xx), tc) for xx in range(2)]
        for c in range(C):
            one, two = got(W * C + 2 * c), got(W * C + 2 * c + 1)
            rows, lanes = [], []
            for p in range(2):
                e, o = one[8 * p : 8 * p + 8], two[8 * p : 8 * p + 8]
                lt, ht = jnp.where(ev8, o, e), jnp.where(ev8, e, o)
                rows.append(jnp.where(sub < 4, lt, pltpu.roll(ht, 4, 0)))
                rows.append(jnp.where(sub < 4, pltpu.roll(lt, 4, 0), ht))
                for xx in range(2):
                    lanes.append(mt * t_unpack(turned[xx], p + 2 * c))
            for i in range(W):
                row = x_halo(rows, i, low, fc)
                bs[c, i] = r_halo(row, row, 0, 1, rc)
                gs[c, i] = x_halo(lanes, i, low, fc)
        for i in range(W):
            q = [state[c, at + i] for c in range(C)]
            out = pull_rt(q, prims(q), [bs[c, i] for c in range(C)], [gs[c, i] for c in range(C)])
            for c in range(C):
                ab[side, c, i] = arim[side, c, i] + out[c]
        put(ab, aout, side, 2)
    for move in moves:
        move.wait()


def near(value):
    return pltpu.with_memory_space_constraint(value, pltpu.VMEM)


LIMIT = pltpu.CompilerParams(vmem_limit_bytes=24 << 20)
FULL = (C, NX, NR, NT)
XPAY = (3 * C, W, NR, NT)
XPAY2 = ((W + 2) * C + 2, NR, NT)
RPAY = (C, NX + 4, 8, NT)
TPAY = (4 * C + 4, NR, NT)
RIM = (2, C, W, NR, NT)
RIM_PAIRS = (0, 1, NX // 2 - 2, NX // 2 - 1)


def call(kernel, smem, vmem, outs, scratch=()):
    run = pl.pallas_call(
        kernel,
        in_specs=[SM] * len(smem) + [VM] * len(vmem),
        out_specs=[VM] * len(outs),
        out_shape=[pltpu.VMEM(s, F32) for s in outs],
        scratch_shapes=list(scratch),
        compiler_params=LIMIT,
    )
    return run(*smem, *[near(v) for v in vmem])


def swap(value, axis, odd):
    count = lax.axis_size(axis)
    pairs = []
    for i in range(odd, count - 1, 2):
        pairs += [(i, i + 1), (i + 1, i)]
    return lax.ppermute(value, axis, pairs)


def across(value):
    return lax.ppermute(value, "th", [(0, 1), (1, 0)])


SPLIT = [pltpu.VMEM((NX, C, NR, NT), BF16), pltpu.VMEM((NX, C, NR, NT), BF16), pltpu.VMEM((NX, C, NR, NT), F32)]
WIDE_R = pltpu.VMEM((C, NX, 32, NT), F32)


def shards(state, seed, cx, cr, ct, cf, met):
    shapes = [FULL, FULL, RIM, XPAY, XPAY]
    state, seed, prim, xe, xo = pl.pallas_call(
        first,
        in_specs=[pl.BlockSpec(memory_space=pltpu.HBM)] * 3,
        out_specs=[VM] * len(shapes),
        out_shape=[pltpu.VMEM(s, F32) for s in shapes],
        scratch_shapes=[pltpu.SMEM((TAPS,), F32), pltpu.SemaphoreType.DMA((3,))],
        name="first",
        compiler_params=LIMIT,
    )(*[pltpu.with_memory_space_constraint(v, pltpu.HBM) for v in (cf, state, seed)])
    xe = swap(xe, "gx", 0)
    xo = swap(xo, "gx", 1)
    plam, re, ro, th = call(second, [cf, met], [state, seed, prim], [FULL, RPAY, RPAY, TPAY])
    th = across(th)
    re = swap(re, "row", 0)
    ro = swap(ro, "row", 1)
    (psec,) = call(
        own, [cx, cr, ct, met], [state], [FULL], [pltpu.VMEM(FULL, F32), WIDE_R] + SPLIT
    )
    srim, lrim, lamh, xe2, xo2 = call(
        join,
        [cx, cr, ct, cf, met],
        [seed, psec, plam, xe, xo, re, ro, th],
        [RIM, RIM, RIM, XPAY2, XPAY2],
    )
    xe2 = swap(xe2, "gx", 0)
    xo2 = swap(xo2, "gx", 1)
    full = pltpu.VMEM(FULL, F32)
    inner = pltpu.VMEM((C, NX - 2 * W, NR, NT), F32)
    whole = jax.ShapeDtypeStruct(FULL, F32)
    new, adj, nrim, arim = pl.pallas_call(
        finish,
        in_specs=[SM] * 5 + [VM] * 9,
        out_specs=[ANY, ANY, VM, VM],
        out_shape=[whole, whole, pltpu.VMEM(RIM, F32), pltpu.VMEM(RIM, F32)],
        scratch_shapes=[full, full, pltpu.VMEM((2, C, NR, NT), F32), WIDE_R]
        + SPLIT
        + [inner, inner, pltpu.SemaphoreType.DMA((2,))],
        name="finish",
        compiler_params=LIMIT,
    )(cx, cr, ct, cf, met, *map(near, (state, psec, plam, srim, lrim, lamh, re, ro, th)))
    return pl.pallas_call(
        edges,
        in_specs=[SM] * 4 + [VM] * 5 + [ANY] * 2,
        out_specs=[ANY, ANY],
        out_shape=[whole, whole],
        scratch_shapes=[pltpu.VMEM(RIM, F32)] * 2
        + [pltpu.VMEM((C, W, NR, NT), F32)] * 2
        + [pltpu.SemaphoreType.DMA((4,))],
        input_output_aliases={9: 0, 10: 1},
        name="edges",
        compiler_params=LIMIT,
    )(cr, ct, cf, met, *map(near, (state, xe2, xo2, nrim, arim)), new, adj)


def solution(mesh):
    whole = P(None, "gx", "row", "th")

    return jax.shard_map(
        shards,
        mesh=mesh,
        in_specs=(whole, whole, P(), P(), P(), P(), P("row")),
        out_specs=(whole, whole),
        check_vma=False,
    )
```

```python
import jax
import jax.numpy as jnp
from jax import lax
from jax.experimental import pallas as pl
from jax.experimental.pallas import tpu as pltpu
from jax.sharding import PartitionSpec as P


DT = 0.1
GAM = 0.4
W = 4
TAPS = 9
C = 5
NX, NR, NT = 32, 16, 128
F32 = jnp.float32
BF16 = jnp.bfloat16
VM = pl.BlockSpec(memory_space=pltpu.VMEM)
SM = pl.BlockSpec(memory_space=pltpu.SMEM)
ANY = pl.BlockSpec(memory_space=pl.ANY)


def prims(q):
    inv = 1.0 / q[0]
    u, v, w = q[1] * inv, q[2] * inv, q[3] * inv
    p = GAM * (q[4] - 0.5 * (q[1] * u + q[2] * v + q[3] * w))
    return inv, u, v, w, p, q[4] + p


def flux_x(q, pr):
    _, u, _, _, p, h = pr
    return [q[1], q[1] * u + p, q[2] * u, q[3] * u, h * u]


def flux_r(q, pr):
    _, _, v, _, p, h = pr
    return [q[2], q[1] * v, q[2] * v + p, q[3] * v, h * v]


def flux_t(q, pr):
    _, _, _, w, p, h = pr
    return [q[3], q[1] * w, q[2] * w, q[3] * w + p, h * w]


def pull(q, pr, a, b, c):
    inv, u, v, w, _, h = pr
    ub = a[1] * q[1] + a[2] * q[2] + a[3] * q[3] + a[4] * h
    vb = b[1] * q[1] + b[2] * q[2] + b[3] * q[3] + b[4] * h
    wb = c[1] * q[1] + c[2] * q[2] + c[3] * q[3] + c[4] * h
    hb = a[4] * u + b[4] * v + c[4] * w
    pb = a[1] + b[2] + c[3] + hb
    s = (-0.5 * GAM) * pb
    ub = (ub + s * q[1]) * inv
    vb = (vb + s * q[2]) * inv
    wb = (wb + s * q[3]) * inv
    o1 = a[0] + (a[1] + s) * u + b[1] * v + c[1] * w + ub
    o2 = b[0] + a[2] * u + (b[2] + s) * v + c[2] * w + vb
    o3 = c[0] + a[3] * u + b[3] * v + (c[3] + s) * w + wb
    o4 = hb + GAM * pb
    o0 = -(ub * u + vb * v + wb * w)
    return [o0, o1, o2, o3, o4]


def pull_rt(q, pr, b, c):
    inv, u, v, w, _, h = pr
    hb = b[4] * v + c[4] * w
    pb = b[2] + c[3] + hb
    s = (-0.5 * GAM) * pb
    ub = s * u
    vb = (b[1] * q[1] + b[2] * q[2] + b[3] * q[3] + b[4] * h + s * q[2]) * inv
    wb = (c[1] * q[1] + c[2] * q[2] + c[3] * q[3] + c[4] * h + s * q[3]) * inv
    o1 = s * u + b[1] * v + c[1] * w + ub
    o2 = b[0] + (b[2] + s) * v + c[2] * w + vb
    o3 = c[0] + b[3] * v + (c[3] + s) * w + wb
    o4 = hb + GAM * pb
    o0 = -(ub * u + vb * v + wb * w)
    return [o0, o1, o2, o3, o4]


def iota(shape, dim):
    return lax.broadcasted_iota(jnp.int32, shape, dim)


def metric_tile(met):
    row = iota((NR, NT), 0)
    tile = jnp.zeros((NR, NT), F32)
    for r in range(NR):
        tile = jnp.where(row == r, met[r], tile)
    return tile


def parity(axis):
    return lax.axis_index(axis) % 2


def is_even(axis):
    return jnp.full((NR, NT), parity(axis), jnp.int32) == 0


def split(x):
    hi = x.astype(BF16)
    return hi, (x - hi.astype(F32)).astype(BF16)


def band(coef):
    offset = iota((NT, NT), 0) - iota((NT, NT), 1) + W
    mat = jnp.zeros((NT, NT), F32)
    for j in range(TAPS):
        mat = jnp.where(offset == j, coef[j], mat)
    return mat


def t_own(hi, lo, coef, out):
    bhi, blo = split(band(coef))
    mat = jnp.concatenate([bhi, bhi, blo], axis=0)
    step = 8
    for g in range(NX // step):
        h = hi[pl.ds(g * step, step)].reshape(step * C * NR, NT)
        l = lo[pl.ds(g * step, step)].reshape(step * C * NR, NT)
        total = jnp.dot(jnp.concatenate([h, l, h], axis=1), mat, preferred_element_type=F32)
        out[pl.ds(g * step, step)] = total.reshape(step, C, NR, NT)


def t_pack_coefs(coef):
    lane = iota((NR, NT), 1) % 8
    masks = {}
    for j in range(W):
        masks[j] = jnp.where((lane >= 4) & (lane < 8 - j), coef[j], 0.0)
    for j in range(W + 1, TAPS):
        masks[j] = jnp.where((lane >= 8 - j) & (lane < 4), coef[j], 0.0)
    return masks


def t_halo_packed(rims, masks):
    total = None
    for j, m in masks.items():
        term = m * pltpu.roll(rims, (4 - j) % NT, 1)
        total = term if total is None else total + term
    return total


def t_unpack(packed, k):
    lane = iota((NR, NT), 1)
    moved = pltpu.roll(packed, 124 - 8 * k, 1)
    return jnp.where((lane < 4) | (lane >= 124), moved, 0.0)


def t_pack_one(ref, at, field, k):
    moved = pltpu.roll(field, (8 * k + 4) % NT, 1)
    ref[at] = jnp.where(lane_block() == k, moved, ref[at])


def lane_block():
    return lax.shift_right_logical(iota((NR, NT), 1), 3)


def t_pack_into(ref, base, fields, xx, k):
    for c in range(C):
        t_pack_one(ref, base + 2 * c + xx, fields[c], k)


def r_pack(first, second, even):
    sub = iota((8, NT), 0)
    low = jnp.where(sub < 4, first[:8], pltpu.roll(second[:8], 4, 0))
    high = jnp.where(sub < 4, pltpu.roll(first[8:], 4, 0), second[8:])
    ev = even[:8]
    return jnp.where(ev, high, low), jnp.where(ev, low, high)


def r_coefs(coef):
    sub = iota((8, NT), 0)
    low = [jnp.where(sub < 4 - j, coef[j], 0.0) for j in range(W)]
    high = {j: jnp.where(sub >= 12 - j, coef[j], 0.0) for j in range(W + 1, TAPS)}
    return low, high


def r_halo(low, high, xlo, xhi, coefs):
    lo_c, hi_c = coefs
    top = None
    for j in range(W):
        shift = (8 - (4 * xlo + j)) % 8
        term = lo_c[j] * (pltpu.roll(low, shift, 0) if shift else low)
        top = term if top is None else top + term
    bottom = None
    for j in range(W + 1, TAPS):
        shift = (12 - j - 4 * xhi) % 8
        term = hi_c[j] * (pltpu.roll(high, shift, 0) if shift else high)
        bottom = term if bottom is None else bottom + term
    return jnp.concatenate([top, bottom], axis=0)


def x_taps(read, x, coef):
    total = None
    for j in range(TAPS):
        at = x + j - W
        if isinstance(x, int) and not 0 <= at < NX:
            continue
        term = coef[j] * read(at)
        total = term if total is None else total + term
    return total


def x_halo(planes, i, low, coef):
    total = None
    for j in range(TAPS):
        at = i + j if low else i + j - 8
        if not 0 <= at < W:
            continue
        term = coef[j] * planes[at]
        total = term if total is None else total + term
    return total


def over_planes(body):
    for x in range(W):
        body(x)

    def step(x, carry):
        body(x)
        return carry

    lax.fori_loop(W, NX - W, step, 0)
    for x in range(NX - W, NX):
        body(x)


def loop(lo, hi, body, unroll=1):
    def step(k, carry):
        body(k)
        return carry

    lax.fori_loop(lo, hi, step, 0, unroll=unroll)


def rim_starts():
    even = parity("gx") == 0
    return jnp.where(even, NX - W, 0), jnp.where(even, 0, NX - W)


def first(cf_hbm, state_hbm, seed_hbm, state, seed, prim, xe, xo, cf, sems):
    moves = [
        pltpu.make_async_copy(seed_hbm, seed, sems.at[0]),
        pltpu.make_async_copy(state_hbm, state, sems.at[1]),
        pltpu.make_async_copy(cf_hbm, cf, sems.at[2]),
    ]
    for move in moves:
        move.start()
    moves[2].wait()
    fc = [-cf[TAPS - 1 - j] for j in range(TAPS)]
    moves[0].wait()
    for side, base in enumerate((0, NX - W)):
        for i in range(W):
            for c in range(C):
                prim[side, c, i] = seed[c, base + i] + x_taps(lambda at: seed[c, at], base + i, fc)
    starts = rim_starts()
    even = parity("gx") == 0
    sides = jnp.where(even, 1, 0), jnp.where(even, 0, 1)
    moves[1].wait()
    for start, side, out in zip(starts, sides, (xe, xo)):
        for i in range(W):
            q = [state[c, start + i] for c in range(C)]
            f = flux_x(q, prims(q))
            for c in range(C):
                out[c, i] = f[c]
                out[C + c, i] = seed[c, start + i]
                out[2 * C + c, i] = prim[side, c, i]


def second(cf, met, state, seed, prim, plam, re, ro, th):
    fc = [-cf[TAPS - 1 - j] for j in range(TAPS)]
    mt = metric_tile(met)
    even = is_even("row")
    th[...] = jnp.zeros(th.shape, F32)
    for side, base in enumerate((0, NX - W)):
        for i in range(W):
            for c in range(C):
                plam[c, base + i] = prim[side, c, i]

    def plane(x):
        for c in range(C):
            plam[c, x] = seed[c, x] + x_taps(lambda at: seed[c, at], x, fc)

    loop(W, NX - W, plane, 2)

    def pair(k):
        keep = []
        for xx in range(2):
            q = [state[c, 2 * k + xx] for c in range(C)]
            pr = prims(q)
            keep.append(flux_r(q, pr))
            t_pack_into(th, 0, flux_t(q, pr), xx, k)
            t_pack_into(th, 2 * C, [mt * plam[c, 2 * k + xx] for c in range(C)], xx, k)
        for c in range(C):
            re[c, k], ro[c, k] = r_pack(keep[0][c], keep[1][c], even)
            at = NX // 2 + k
            re[c, at], ro[c, at] = r_pack(plam[c, 2 * k], plam[c, 2 * k + 1], even)

    loop(0, NX // 2, pair, 2)
    for n, k in enumerate(RIM_PAIRS):
        for c in range(C):
            at = NX + n
            re[c, at], ro[c, at] = r_pack(seed[c, 2 * k], seed[c, 2 * k + 1], even)
            for xx in range(2):
                t_pack_one(th, 4 * C + 2 * (n // 2) + xx, seed[c, 2 * k + xx], n % 2 + 2 * c)


def own(cx, cr, ct, met, state, psec, fx, fr, hi, lo, tt):
    mt = metric_tile(met)
    zero = jnp.zeros((8, NT), F32)

    def fill(x):
        q = [state[c, x] for c in range(C)]
        pr = prims(q)
        f, g, h = flux_x(q, pr), flux_r(q, pr), flux_t(q, pr)
        for c in range(C):
            fx[c, x] = f[c]
            fr[c, x, 0:8] = zero
            fr[c, x, 8:24] = g[c]
            fr[c, x, 24:32] = zero
            hi[x, c], lo[x, c] = split(h[c])

    loop(0, NX, fill)
    t_own(hi, lo, [-DT * ct[j] for j in range(TAPS)], tt)
    xc = [-DT * cx[j] for j in range(TAPS)]
    rc = [-DT * cr[j] for j in range(TAPS)]

    def plane(x):
        for c in range(C):
            acc = state[c, x] + mt * tt[x, c]
            acc += x_taps(lambda at: fx[c, at], x, xc)
            for j in range(TAPS):
                acc += rc[j] * fr[c, x, 4 + j : 20 + j]
            psec[c, x] = acc

    over_planes(plane)


def join(even_side, cx, cr, ct, cf, met, seed, psec, plam, x, re, ro, th, srim, lrim, lamh, x2):
    mt = metric_tile(met)
    ev8 = is_even("row")[:8]
    fc = [-cf[TAPS - 1 - j] for j in range(TAPS)]
    xc = [-DT * cx[j] for j in range(TAPS)]
    place = jnp.full((NR, NT), lax.axis_index("gx"), jnp.int32)
    has = place > 0, place < lax.axis_size("gx") - 1
    share = rt_share(cr, ct, mt, ev8, re, ro, th)

    def at_side(side):
        low, base = side == 0, (0, NX - W)[side]
        for c in range(C):
            flux = [x[c, i] for i in range(W)]
            seeds = [x[C + c, i] for i in range(W)]
            mine = [seed[c, base + i] for i in range(W)]
            both = []
            for p in range(2):
                both += share(c, RIM_PAIRS[2 * side + p])
            for i in range(W):
                value = psec[c, base + i] + x_halo(flux, i, low, xc) + both[i]
                srim[c, i] = value
                x2[W * c + i] = value
                lrim[c, i] = plam[c, base + i] + x_halo(seeds, i, low, fc)
                value = x[2 * C + c, i] + x_halo(mine, i, not low, fc)
                lamh[c, i] = jnp.where(has[side], value, 0.0)
            for eo, src in enumerate((re, ro)):
                for p in range(2):
                    x2[W * C + 2 * c + eo, 8 * p : 8 * p + 8] = src[c, NX + 2 * side + p]
        for xx in range(2):
            x2[(W + 2) * C + xx] = th[4 * C + 2 * side + xx]

    even = parity("gx") == 0
    pl.when(even)(lambda: at_side(even_side))
    pl.when(jnp.logical_not(even))(lambda: at_side(1 - even_side))


def join_e(*refs):
    join(1, *refs)


def join_o(*refs):
    join(0, *refs)


def rt_share(cr, ct, mt, ev8, re, ro, th):
    rc = r_coefs([-DT * cr[j] for j in range(TAPS)])
    tc = t_pack_coefs([-DT * ct[j] for j in range(TAPS)])
    packed = [[mt * t_halo_packed(th[2 * c + xx], tc) for xx in range(2)] for c in range(C)]

    def share(c, k):
        a, b = re[c, k], ro[c, k]
        low, high = jnp.where(ev8, b, a), jnp.where(ev8, a, b)
        return [r_halo(low, high, xx, xx, rc) + t_unpack(packed[c][xx], k) for xx in range(2)]

    return share


def finish(
    cx, cr, ct, cf, met, state, psec, plam, se, so, le, lo_, lhe, lho, re, ro, th,
    new, adj, nrim, arim, sec, lam, pk, lr, hi, lo, tt, nb, ab, sems,
):
    mt = metric_tile(met)
    evr = is_even("row")
    ev8 = evr[:8]
    rx = [-DT * cx[TAPS - 1 - j] for j in range(TAPS)]
    rr = [-DT * cr[TAPS - 1 - j] for j in range(TAPS)]
    rt = [-DT * ct[TAPS - 1 - j] for j in range(TAPS)]
    tc = t_pack_coefs(rt)
    evx = is_even("gx")

    def pick(side, e, o, c, i):
        mine, other = (o, e) if side == 0 else (e, o)
        return jnp.where(evx, mine[c, i], other[c, i])

    for c in range(C):
        for xx in range(2):
            pk[xx, c] = t_halo_packed(th[2 * C + 2 * c + xx], tc)
        for side, base in enumerate((0, NX - W)):
            for i in range(W):
                sec[c, base + i] = pick(side, se, so, c, i)
                lam[c, base + i] = pick(side, le, lo_, c, i)
    share = rt_share(cr, ct, mt, ev8, re, ro, th)

    def inner(k):
        for c in range(C):
            for xx, value in enumerate(share(c, k)):
                x = 2 * k + xx
                sec[c, x] = psec[c, x] + value
                lam[c, x] = plam[c, x]

    loop(2, 14, inner)

    def fill(k):
        for c in range(C):
            at = NX // 2 + k
            a, b = re[c, at], ro[c, at]
            low, high = jnp.where(ev8, b, a), jnp.where(ev8, a, b)
            for xx in range(2):
                x = 2 * k + xx
                value = lam[c, x]
                lr[c, x, 0:8] = low if xx else pltpu.roll(low, 4, 0)
                lr[c, x, 8:24] = value
                lr[c, x, 24:32] = pltpu.roll(high, 4, 0) if xx else high
                hi[x, c], lo[x, c] = split(mt * value)

    loop(0, NX // 2, fill)
    t_own(hi, lo, rt, tt)

    fcs = [cf[j] for j in range(TAPS)]

    def plane(x):
        q = [state[c, x] for c in range(C)]
        pr = prims(q)
        rim = isinstance(x, int)
        side, at = (0, x) if rim and x < W else (1, x - NX + W)
        a, b, g = [], [], []
        for c in range(C):
            acc = x_taps(lambda at: lam[c, at], x, rx)
            if rim:
                acc += x_halo([pick(side, lhe, lho, c, h) for h in range(W)], at, side == 0, rx)
            a.append(acc)
            acc = None
            for j in range(TAPS):
                term = rr[j] * lr[c, x, 4 + j : 20 + j]
                acc = term if acc is None else acc + term
            b.append(acc)
            g.append(tt[x, c] + t_unpack(pk[x % 2, c], x // 2))
        out = pull(q, pr, a, b, g)
        for c in range(C):
            av = lam[c, x] + out[c]
            nv = sec[c, x] - x_taps(lambda at: sec[c, at], x, fcs)
            if rim:
                arim[side, c, at], nrim[side, c, at] = av, nv
            else:
                ab[c, x - W], nb[c, x - W] = av, nv

    lax.fori_loop(W, NX - W, lambda x, carry: (plane(x), carry)[1], 0)
    inside = pl.ds(W, NX - 2 * W)
    moves = [
        pltpu.make_async_copy(ab, adj.at[:, inside], sems.at[0]),
        pltpu.make_async_copy(nb, new.at[:, inside], sems.at[1]),
    ]
    for move in moves:
        move.start()
    for x in (*range(W), *range(NX - W, NX)):
        plane(x)
    for move in moves:
        move.wait()


def edges(cr, ct, cf, met, state, xe2, xo2, nrim, arim, nin, ain, nout, aout, nb, ab, bs, gs, sems):
    mt = metric_tile(met)
    evx, evr = is_even("gx"), is_even("row")
    ev8 = evr[:8]
    sub = iota((8, NT), 0)
    fc = [-cf[TAPS - 1 - j] for j in range(TAPS)]
    fcs = [cf[j] for j in range(TAPS)]
    rc = r_coefs([-DT * cr[TAPS - 1 - j] for j in range(TAPS)])
    tc = t_pack_coefs([-DT * ct[TAPS - 1 - j] for j in range(TAPS)])
    starts = (0, NX - W)
    moves = []

    def put(buf, dst, side, slot):
        move = pltpu.make_async_copy(
            buf.at[side], dst.at[:, pl.ds(starts[side], W)], sems.at[slot + side]
        )
        move.start()
        moves.append(move)

    for side, at in enumerate(starts):
        low = side == 0
        mine, other = (xo2, xe2) if low else (xe2, xo2)

        def got(n):
            return jnp.where(evx, mine[n], other[n])

        for c in range(C):
            planes = [got(W * c + i) for i in range(W)]
            for i in range(W):
                nb[side, c, i] = nrim[side, c, i] - x_halo(planes, i, low, fcs)
        put(nb, nout, side, 0)
        turned = [t_halo_packed(got((W + 2) * C + xx), tc) for xx in range(2)]
        for c in range(C):
            one, two = got(W * C + 2 * c), got(W * C + 2 * c + 1)
            rows, lanes = [], []
            for p in range(2):
                e, o = one[8 * p : 8 * p + 8], two[8 * p : 8 * p + 8]
                lt, ht = jnp.where(ev8, o, e), jnp.where(ev8, e, o)
                rows.append(jnp.where(sub < 4, lt, pltpu.roll(ht, 4, 0)))
                rows.append(jnp.where(sub < 4, pltpu.roll(lt, 4, 0), ht))
                for xx in range(2):
                    lanes.append(mt * t_unpack(turned[xx], p + 2 * c))
            for i in range(W):
                row = x_halo(rows, i, low, fc)
                bs[c, i] = r_halo(row, row, 0, 1, rc)
                gs[c, i] = x_halo(lanes, i, low, fc)
        for i in range(W):
            q = [state[c, at + i] for c in range(C)]
            out = pull_rt(q, prims(q), [bs[c, i] for c in range(C)], [gs[c, i] for c in range(C)])
            for c in range(C):
                ab[side, c, i] = arim[side, c, i] + out[c]
        put(ab, aout, side, 2)
    for move in moves:
        move.wait()


def near(value):
    return pltpu.with_memory_space_constraint(value, pltpu.VMEM)


LIMIT = pltpu.CompilerParams(vmem_limit_bytes=24 << 20)
FULL = (C, NX, NR, NT)
XPAY = (3 * C, W, NR, NT)
XPAY2 = ((W + 2) * C + 2, NR, NT)
RPAY = (C, NX + 4, 8, NT)
TPAY = (4 * C + 4, NR, NT)
RIM = (2, C, W, NR, NT)
RIM_PAIRS = (0, 1, NX // 2 - 2, NX // 2 - 1)


def call(kernel, smem, vmem, outs, scratch=()):
    run = pl.pallas_call(
        kernel,
        in_specs=[SM] * len(smem) + [VM] * len(vmem),
        out_specs=[VM] * len(outs),
        out_shape=[pltpu.VMEM(s, F32) for s in outs],
        scratch_shapes=list(scratch),
        compiler_params=LIMIT,
    )
    return run(*smem, *[near(v) for v in vmem])


def swap(value, axis, odd):
    count = lax.axis_size(axis)
    pairs = []
    for i in range(odd, count - 1, 2):
        pairs += [(i, i + 1), (i + 1, i)]
    return lax.ppermute(value, axis, pairs)


def across(value):
    return lax.ppermute(value, "th", [(0, 1), (1, 0)])


SPLIT = [pltpu.VMEM((NX, C, NR, NT), BF16), pltpu.VMEM((NX, C, NR, NT), BF16), pltpu.VMEM((NX, C, NR, NT), F32)]
WIDE_R = pltpu.VMEM((C, NX, 32, NT), F32)


def shards(state, seed, cx, cr, ct, cf, met):
    shapes = [FULL, FULL, RIM, XPAY, XPAY]
    state, seed, prim, xe, xo = pl.pallas_call(
        first,
        in_specs=[pl.BlockSpec(memory_space=pltpu.HBM)] * 3,
        out_specs=[VM] * len(shapes),
        out_shape=[pltpu.VMEM(s, F32) for s in shapes],
        scratch_shapes=[pltpu.SMEM((TAPS,), F32), pltpu.SemaphoreType.DMA((3,))],
        name="first",
        compiler_params=LIMIT,
    )(*[pltpu.with_memory_space_constraint(v, pltpu.HBM) for v in (cf, state, seed)])
    xe = swap(xe, "gx", 0)
    xo = swap(xo, "gx", 1)
    plam, re, ro, th = call(second, [cf, met], [state, seed, prim], [FULL, RPAY, RPAY, TPAY])
    th = across(th)
    re = swap(re, "row", 0)
    ro = swap(ro, "row", 1)
    (psec,) = call(own, [cx, cr, ct, met], [state], [FULL], [pltpu.VMEM(FULL, F32), WIDE_R] + SPLIT)
    one = [(C, W, NR, NT)] * 3 + [XPAY2]
    near_args = [seed, psec, plam]
    se, le, lhe, xe2 = call(join_e, [cx, cr, ct, cf, met], near_args + [xe, re, ro, th], one)
    xe2 = swap(xe2, "gx", 0)
    so, lo, lho, xo2 = call(join_o, [cx, cr, ct, cf, met], near_args + [xo, re, ro, th], one)
    xo2 = swap(xo2, "gx", 1)
    full = pltpu.VMEM(FULL, F32)
    inner = pltpu.VMEM((C, NX - 2 * W, NR, NT), F32)
    whole = jax.ShapeDtypeStruct(FULL, F32)
    new, adj, nrim, arim = pl.pallas_call(
        finish,
        in_specs=[SM] * 5 + [VM] * 12,
        out_specs=[ANY, ANY, VM, VM],
        out_shape=[whole, whole, pltpu.VMEM(RIM, F32), pltpu.VMEM(RIM, F32)],
        scratch_shapes=[full, full, pltpu.VMEM((2, C, NR, NT), F32), WIDE_R]
        + SPLIT
        + [inner, inner, pltpu.SemaphoreType.DMA((2,))],
        name="finish",
        compiler_params=LIMIT,
    )(cx, cr, ct, cf, met, *map(near, (state, psec, plam, se, so, le, lo, lhe, lho, re, ro, th)))
    return pl.pallas_call(
        edges,
        in_specs=[SM] * 4 + [VM] * 5 + [ANY] * 2,
        out_specs=[ANY, ANY],
        out_shape=[whole, whole],
        scratch_shapes=[pltpu.VMEM(RIM, F32)] * 2
        + [pltpu.VMEM((C, W, NR, NT), F32)] * 2
        + [pltpu.SemaphoreType.DMA((4,))],
        input_output_aliases={9: 0, 10: 1},
        name="edges",
        compiler_params=LIMIT,
    )(cr, ct, cf, met, *map(near, (state, xe2, xo2, nrim, arim)), new, adj)


def solution(mesh):
    whole = P(None, "gx", "row", "th")

    return jax.shard_map(
        shards,
        mesh=mesh,
        in_specs=(whole, whole, P(), P(), P(), P(), P("row")),
        out_specs=(whole, whole),
        check_vma=False,
    )
```

```python
import jax
import jax.numpy as jnp
from jax import lax
from jax.experimental import pallas as pl
from jax.experimental.pallas import tpu as pltpu
from jax.sharding import PartitionSpec as P


DT = 0.1
GAM = 0.4
W = 4
TAPS = 9
C = 5
NX, NR, NT = 32, 16, 128
F32 = jnp.float32
BF16 = jnp.bfloat16
VM = pl.BlockSpec(memory_space=pltpu.VMEM)
SM = pl.BlockSpec(memory_space=pltpu.SMEM)
ANY = pl.BlockSpec(memory_space=pl.ANY)


def prims(q):
    inv = 1.0 / q[0]
    u, v, w = q[1] * inv, q[2] * inv, q[3] * inv
    p = GAM * (q[4] - 0.5 * (q[1] * u + q[2] * v + q[3] * w))
    return inv, u, v, w, p, q[4] + p


def flux_x(q, pr):
    _, u, _, _, p, h = pr
    return [q[1], q[1] * u + p, q[2] * u, q[3] * u, h * u]


def flux_r(q, pr):
    _, _, v, _, p, h = pr
    return [q[2], q[1] * v, q[2] * v + p, q[3] * v, h * v]


def flux_t(q, pr):
    _, _, _, w, p, h = pr
    return [q[3], q[1] * w, q[2] * w, q[3] * w + p, h * w]


def pull(q, pr, a, b, c):
    inv, u, v, w, _, h = pr
    ub = a[1] * q[1] + a[2] * q[2] + a[3] * q[3] + a[4] * h
    vb = b[1] * q[1] + b[2] * q[2] + b[3] * q[3] + b[4] * h
    wb = c[1] * q[1] + c[2] * q[2] + c[3] * q[3] + c[4] * h
    hb = a[4] * u + b[4] * v + c[4] * w
    pb = a[1] + b[2] + c[3] + hb
    s = (-0.5 * GAM) * pb
    ub = (ub + s * q[1]) * inv
    vb = (vb + s * q[2]) * inv
    wb = (wb + s * q[3]) * inv
    o1 = a[0] + (a[1] + s) * u + b[1] * v + c[1] * w + ub
    o2 = b[0] + a[2] * u + (b[2] + s) * v + c[2] * w + vb
    o3 = c[0] + a[3] * u + b[3] * v + (c[3] + s) * w + wb
    o4 = hb + GAM * pb
    o0 = -(ub * u + vb * v + wb * w)
    return [o0, o1, o2, o3, o4]


def pull_rt(q, pr, b, c):
    inv, u, v, w, _, h = pr
    hb = b[4] * v + c[4] * w
    pb = b[2] + c[3] + hb
    s = (-0.5 * GAM) * pb
    ub = s * u
    vb = (b[1] * q[1] + b[2] * q[2] + b[3] * q[3] + b[4] * h + s * q[2]) * inv
    wb = (c[1] * q[1] + c[2] * q[2] + c[3] * q[3] + c[4] * h + s * q[3]) * inv
    o1 = s * u + b[1] * v + c[1] * w + ub
    o2 = b[0] + (b[2] + s) * v + c[2] * w + vb
    o3 = c[0] + b[3] * v + (c[3] + s) * w + wb
    o4 = hb + GAM * pb
    o0 = -(ub * u + vb * v + wb * w)
    return [o0, o1, o2, o3, o4]


def iota(shape, dim):
    return lax.broadcasted_iota(jnp.int32, shape, dim)


def metric_tile(met):
    row = iota((NR, NT), 0)
    tile = jnp.zeros((NR, NT), F32)
    for r in range(NR):
        tile = jnp.where(row == r, met[r], tile)
    return tile


def parity(axis):
    return lax.axis_index(axis) % 2


def is_even(axis):
    return jnp.full((NR, NT), parity(axis), jnp.int32) == 0


def split(x):
    hi = x.astype(BF16)
    return hi, (x - hi.astype(F32)).astype(BF16)


def band(coef):
    offset = iota((NT, NT), 0) - iota((NT, NT), 1) + W
    mat = jnp.zeros((NT, NT), F32)
    for j in range(TAPS):
        mat = jnp.where(offset == j, coef[j], mat)
    return mat


def t_own(hi, lo, coef, out):
    bhi, blo = split(band(coef))
    mat = jnp.concatenate([bhi, bhi, blo], axis=0)
    step = 8
    for g in range(NX // step):
        h = hi[pl.ds(g * step, step)].reshape(step * C * NR, NT)
        l = lo[pl.ds(g * step, step)].reshape(step * C * NR, NT)
        total = jnp.dot(jnp.concatenate([h, l, h], axis=1), mat, preferred_element_type=F32)
        out[pl.ds(g * step, step)] = total.reshape(step, C, NR, NT)


def t_pack_coefs(coef):
    lane = iota((NR, NT), 1) % 8
    masks = {}
    for j in range(W):
        masks[j] = jnp.where((lane >= 4) & (lane < 8 - j), coef[j], 0.0)
    for j in range(W + 1, TAPS):
        masks[j] = jnp.where((lane >= 8 - j) & (lane < 4), coef[j], 0.0)
    return masks


def t_halo_packed(rims, masks):
    total = None
    for j, m in masks.items():
        term = m * pltpu.roll(rims, (4 - j) % NT, 1)
        total = term if total is None else total + term
    return total


def t_unpack(packed, k):
    lane = iota((NR, NT), 1)
    moved = pltpu.roll(packed, 124 - 8 * k, 1)
    return jnp.where((lane < 4) | (lane >= 124), moved, 0.0)


def t_pack_one(ref, at, field, k):
    moved = pltpu.roll(field, (8 * k + 4) % NT, 1)
    ref[at] = jnp.where(lane_block() == k, moved, ref[at])


def lane_block():
    return lax.shift_right_logical(iota((NR, NT), 1), 3)


def t_pack_into(ref, base, fields, xx, k):
    for c in range(C):
        t_pack_one(ref, base + 2 * c + xx, fields[c], k)


def r_pack(first, second, even):
    sub = iota((8, NT), 0)
    low = jnp.where(sub < 4, first[:8], pltpu.roll(second[:8], 4, 0))
    high = jnp.where(sub < 4, pltpu.roll(first[8:], 4, 0), second[8:])
    ev = even[:8]
    return jnp.where(ev, high, low), jnp.where(ev, low, high)


def r_coefs(coef):
    sub = iota((8, NT), 0)
    low = [jnp.where(sub < 4 - j, coef[j], 0.0) for j in range(W)]
    high = {j: jnp.where(sub >= 12 - j, coef[j], 0.0) for j in range(W + 1, TAPS)}
    return low, high


def r_halo(low, high, xlo, xhi, coefs):
    lo_c, hi_c = coefs
    top = None
    for j in range(W):
        shift = (8 - (4 * xlo + j)) % 8
        term = lo_c[j] * (pltpu.roll(low, shift, 0) if shift else low)
        top = term if top is None else top + term
    bottom = None
    for j in range(W + 1, TAPS):
        shift = (12 - j - 4 * xhi) % 8
        term = hi_c[j] * (pltpu.roll(high, shift, 0) if shift else high)
        bottom = term if bottom is None else bottom + term
    return jnp.concatenate([top, bottom], axis=0)


def x_taps(read, x, coef):
    total = None
    for j in range(TAPS):
        at = x + j - W
        if isinstance(x, int) and not 0 <= at < NX:
            continue
        term = coef[j] * read(at)
        total = term if total is None else total + term
    return total


def x_halo(planes, i, low, coef):
    total = None
    for j in range(TAPS):
        at = i + j if low else i + j - 8
        if not 0 <= at < W:
            continue
        term = coef[j] * planes[at]
        total = term if total is None else total + term
    return total


def over_planes(body):
    for x in range(W):
        body(x)

    def step(x, carry):
        body(x)
        return carry

    lax.fori_loop(W, NX - W, step, 0)
    for x in range(NX - W, NX):
        body(x)


def loop(lo, hi, body, unroll=1):
    def step(k, carry):
        body(k)
        return carry

    lax.fori_loop(lo, hi, step, 0, unroll=unroll)


def rim_starts():
    even = parity("gx") == 0
    return jnp.where(even, NX - W, 0), jnp.where(even, 0, NX - W)


def first(cf_hbm, state_hbm, seed_hbm, state, seed, prim, xe, xo, cf, sems):
    moves = [
        pltpu.make_async_copy(seed_hbm, seed, sems.at[0]),
        pltpu.make_async_copy(state_hbm, state, sems.at[1]),
        pltpu.make_async_copy(cf_hbm, cf, sems.at[2]),
    ]
    for move in moves:
        move.start()
    moves[2].wait()
    fc = [-cf[TAPS - 1 - j] for j in range(TAPS)]
    moves[0].wait()
    for side, base in enumerate((0, NX - W)):
        for i in range(W):
            for c in range(C):
                prim[side, c, i] = seed[c, base + i] + x_taps(lambda at: seed[c, at], base + i, fc)
    starts = rim_starts()
    even = parity("gx") == 0
    sides = jnp.where(even, 1, 0), jnp.where(even, 0, 1)
    moves[1].wait()
    for start, side, out in zip(starts, sides, (xe, xo)):
        for i in range(W):
            q = [state[c, start + i] for c in range(C)]
            f = flux_x(q, prims(q))
            for c in range(C):
                out[c, i] = f[c]
                out[C + c, i] = seed[c, start + i]
                out[2 * C + c, i] = prim[side, c, i]


def second(cf, met, state, seed, prim, plam, re, ro, th):
    fc = [-cf[TAPS - 1 - j] for j in range(TAPS)]
    mt = metric_tile(met)
    even = is_even("row")
    th[...] = jnp.zeros(th.shape, F32)
    for side, base in enumerate((0, NX - W)):
        for i in range(W):
            for c in range(C):
                plam[c, base + i] = prim[side, c, i]

    def plane(x):
        for c in range(C):
            plam[c, x] = seed[c, x] + x_taps(lambda at: seed[c, at], x, fc)

    loop(W, NX - W, plane, 2)

    def pair(k):
        keep = []
        for xx in range(2):
            q = [state[c, 2 * k + xx] for c in range(C)]
            pr = prims(q)
            keep.append(flux_r(q, pr))
            t_pack_into(th, 0, flux_t(q, pr), xx, k)
            t_pack_into(th, 2 * C, [mt * plam[c, 2 * k + xx] for c in range(C)], xx, k)
        for c in range(C):
            re[c, k], ro[c, k] = r_pack(keep[0][c], keep[1][c], even)
            at = NX // 2 + k
            re[c, at], ro[c, at] = r_pack(plam[c, 2 * k], plam[c, 2 * k + 1], even)

    loop(0, NX // 2, pair, 2)
    for n, k in enumerate(RIM_PAIRS):
        for c in range(C):
            at = NX + n
            re[c, at], ro[c, at] = r_pack(seed[c, 2 * k], seed[c, 2 * k + 1], even)
            for xx in range(2):
                t_pack_one(th, 4 * C + 2 * (n // 2) + xx, seed[c, 2 * k + xx], n % 2 + 2 * c)


def own_flux(ct, state, fx, fr, tt, hi, lo):
    zero = jnp.zeros((8, NT), F32)

    def fill(x):
        q = [state[c, x] for c in range(C)]
        pr = prims(q)
        f, g, h = flux_x(q, pr), flux_r(q, pr), flux_t(q, pr)
        for c in range(C):
            fx[c, x] = f[c]
            fr[c, x, 0:8] = zero
            fr[c, x, 8:24] = g[c]
            fr[c, x, 24:32] = zero
            hi[x, c], lo[x, c] = split(h[c])

    loop(0, NX, fill)
    t_own(hi, lo, [-DT * ct[j] for j in range(TAPS)], tt)


def own(cx, cr, met, state, fx, fr, tt, psec):
    mt = metric_tile(met)
    xc = [-DT * cx[j] for j in range(TAPS)]
    rc = [-DT * cr[j] for j in range(TAPS)]

    def plane(x):
        for c in range(C):
            acc = state[c, x] + mt * tt[x, c]
            acc += x_taps(lambda at: fx[c, at], x, xc)
            for j in range(TAPS):
                acc += rc[j] * fr[c, x, 4 + j : 20 + j]
            psec[c, x] = acc

    over_planes(plane)


def join(even_side, cx, cr, ct, cf, met, seed, psec, plam, x, re, ro, th, srim, lrim, lamh, x2):
    mt = metric_tile(met)
    ev8 = is_even("row")[:8]
    fc = [-cf[TAPS - 1 - j] for j in range(TAPS)]
    xc = [-DT * cx[j] for j in range(TAPS)]
    place = jnp.full((NR, NT), lax.axis_index("gx"), jnp.int32)
    has = place > 0, place < lax.axis_size("gx") - 1
    share = rt_share(cr, ct, mt, ev8, re, ro, th)

    def at_side(side):
        low, base = side == 0, (0, NX - W)[side]
        for c in range(C):
            flux = [x[c, i] for i in range(W)]
            seeds = [x[C + c, i] for i in range(W)]
            mine = [seed[c, base + i] for i in range(W)]
            both = []
            for p in range(2):
                both += share(c, RIM_PAIRS[2 * side + p])
            for i in range(W):
                value = psec[c, base + i] + x_halo(flux, i, low, xc) + both[i]
                srim[c, i] = value
                x2[W * c + i] = value
                lrim[c, i] = plam[c, base + i] + x_halo(seeds, i, low, fc)
                value = x[2 * C + c, i] + x_halo(mine, i, not low, fc)
                lamh[c, i] = jnp.where(has[side], value, 0.0)
            for eo, src in enumerate((re, ro)):
                for p in range(2):
                    x2[W * C + 2 * c + eo, 8 * p : 8 * p + 8] = src[c, NX + 2 * side + p]
        for xx in range(2):
            x2[(W + 2) * C + xx] = th[4 * C + 2 * side + xx]

    even = parity("gx") == 0
    pl.when(even)(lambda: at_side(even_side))
    pl.when(jnp.logical_not(even))(lambda: at_side(1 - even_side))


def join_e(*refs):
    join(1, *refs)


def join_o(*refs):
    join(0, *refs)


def rt_share(cr, ct, mt, ev8, re, ro, th):
    rc = r_coefs([-DT * cr[j] for j in range(TAPS)])
    tc = t_pack_coefs([-DT * ct[j] for j in range(TAPS)])
    packed = [[mt * t_halo_packed(th[2 * c + xx], tc) for xx in range(2)] for c in range(C)]

    def share(c, k):
        a, b = re[c, k], ro[c, k]
        low, high = jnp.where(ev8, b, a), jnp.where(ev8, a, b)
        return [r_halo(low, high, xx, xx, rc) + t_unpack(packed[c][xx], k) for xx in range(2)]

    return share


def finish(
    cx, cr, ct, cf, met, state, psec, plam, se, so, le, lo_, lhe, lho, re, ro, th,
    new, adj, nrim, arim, sec, lam, pk, lr, hi, lo, tt, nb, ab, sems,
):
    mt = metric_tile(met)
    evr = is_even("row")
    ev8 = evr[:8]
    rx = [-DT * cx[TAPS - 1 - j] for j in range(TAPS)]
    rr = [-DT * cr[TAPS - 1 - j] for j in range(TAPS)]
    rt = [-DT * ct[TAPS - 1 - j] for j in range(TAPS)]
    tc = t_pack_coefs(rt)
    evx = is_even("gx")

    def pick(side, e, o, c, i):
        mine, other = (o, e) if side == 0 else (e, o)
        return jnp.where(evx, mine[c, i], other[c, i])

    for c in range(C):
        for xx in range(2):
            pk[xx, c] = t_halo_packed(th[2 * C + 2 * c + xx], tc)
        for side, base in enumerate((0, NX - W)):
            for i in range(W):
                sec[c, base + i] = pick(side, se, so, c, i)
                lam[c, base + i] = pick(side, le, lo_, c, i)
    share = rt_share(cr, ct, mt, ev8, re, ro, th)

    def inner(k):
        for c in range(C):
            for xx, value in enumerate(share(c, k)):
                x = 2 * k + xx
                sec[c, x] = psec[c, x] + value
                lam[c, x] = plam[c, x]

    loop(2, 14, inner)

    def fill(k):
        for c in range(C):
            at = NX // 2 + k
            a, b = re[c, at], ro[c, at]
            low, high = jnp.where(ev8, b, a), jnp.where(ev8, a, b)
            for xx in range(2):
                x = 2 * k + xx
                value = lam[c, x]
                lr[c, x, 0:8] = low if xx else pltpu.roll(low, 4, 0)
                lr[c, x, 8:24] = value
                lr[c, x, 24:32] = pltpu.roll(high, 4, 0) if xx else high
                hi[x, c], lo[x, c] = split(mt * value)

    loop(0, NX // 2, fill)
    t_own(hi, lo, rt, tt)

    fcs = [cf[j] for j in range(TAPS)]

    def plane(x):
        q = [state[c, x] for c in range(C)]
        pr = prims(q)
        rim = isinstance(x, int)
        side, at = (0, x) if rim and x < W else (1, x - NX + W)
        a, b, g = [], [], []
        for c in range(C):
            acc = x_taps(lambda at: lam[c, at], x, rx)
            if rim:
                acc += x_halo([pick(side, lhe, lho, c, h) for h in range(W)], at, side == 0, rx)
            a.append(acc)
            acc = None
            for j in range(TAPS):
                term = rr[j] * lr[c, x, 4 + j : 20 + j]
                acc = term if acc is None else acc + term
            b.append(acc)
            g.append(tt[x, c] + t_unpack(pk[x % 2, c], x // 2))
        out = pull(q, pr, a, b, g)
        for c in range(C):
            av = lam[c, x] + out[c]
            nv = sec[c, x] - x_taps(lambda at: sec[c, at], x, fcs)
            if rim:
                arim[side, c, at], nrim[side, c, at] = av, nv
            else:
                ab[c, x - W], nb[c, x - W] = av, nv

    lax.fori_loop(W, NX - W, lambda x, carry: (plane(x), carry)[1], 0)
    inside = pl.ds(W, NX - 2 * W)
    moves = [
        pltpu.make_async_copy(ab, adj.at[:, inside], sems.at[0]),
        pltpu.make_async_copy(nb, new.at[:, inside], sems.at[1]),
    ]
    for move in moves:
        move.start()
    for x in (*range(W), *range(NX - W, NX)):
        plane(x)
    for move in moves:
        move.wait()


def edges(cr, ct, cf, met, state, xe2, xo2, nrim, arim, nin, ain, nout, aout, nb, ab, bs, gs, sems):
    mt = metric_tile(met)
    evx, evr = is_even("gx"), is_even("row")
    ev8 = evr[:8]
    sub = iota((8, NT), 0)
    fc = [-cf[TAPS - 1 - j] for j in range(TAPS)]
    fcs = [cf[j] for j in range(TAPS)]
    rc = r_coefs([-DT * cr[TAPS - 1 - j] for j in range(TAPS)])
    tc = t_pack_coefs([-DT * ct[TAPS - 1 - j] for j in range(TAPS)])
    starts = (0, NX - W)
    moves = []

    def put(buf, dst, side, slot):
        move = pltpu.make_async_copy(
            buf.at[side], dst.at[:, pl.ds(starts[side], W)], sems.at[slot + side]
        )
        move.start()
        moves.append(move)

    for side, at in enumerate(starts):
        low = side == 0
        mine, other = (xo2, xe2) if low else (xe2, xo2)

        def got(n):
            return jnp.where(evx, mine[n], other[n])

        for c in range(C):
            planes = [got(W * c + i) for i in range(W)]
            for i in range(W):
                nb[side, c, i] = nrim[side, c, i] - x_halo(planes, i, low, fcs)
        put(nb, nout, side, 0)
        turned = [t_halo_packed(got((W + 2) * C + xx), tc) for xx in range(2)]
        for c in range(C):
            one, two = got(W * C + 2 * c), got(W * C + 2 * c + 1)
            rows, lanes = [], []
            for p in range(2):
                e, o = one[8 * p : 8 * p + 8], two[8 * p : 8 * p + 8]
                lt, ht = jnp.where(ev8, o, e), jnp.where(ev8, e, o)
                rows.append(jnp.where(sub < 4, lt, pltpu.roll(ht, 4, 0)))
                rows.append(jnp.where(sub < 4, pltpu.roll(lt, 4, 0), ht))
                for xx in range(2):
                    lanes.append(mt * t_unpack(turned[xx], p + 2 * c))
            for i in range(W):
                row = x_halo(rows, i, low, fc)
                bs[c, i] = r_halo(row, row, 0, 1, rc)
                gs[c, i] = x_halo(lanes, i, low, fc)
        for i in range(W):
            q = [state[c, at + i] for c in range(C)]
            out = pull_rt(q, prims(q), [bs[c, i] for c in range(C)], [gs[c, i] for c in range(C)])
            for c in range(C):
                ab[side, c, i] = arim[side, c, i] + out[c]
        put(ab, aout, side, 2)
    for move in moves:
        move.wait()


def near(value):
    return pltpu.with_memory_space_constraint(value, pltpu.VMEM)


LIMIT = pltpu.CompilerParams(vmem_limit_bytes=24 << 20)
FULL = (C, NX, NR, NT)
XPAY = (3 * C, W, NR, NT)
XPAY2 = ((W + 2) * C + 2, NR, NT)
RPAY = (C, NX + 4, 8, NT)
TPAY = (4 * C + 4, NR, NT)
RIM = (2, C, W, NR, NT)
RIM_PAIRS = (0, 1, NX // 2 - 2, NX // 2 - 1)


def call(kernel, smem, vmem, outs, scratch=()):
    run = pl.pallas_call(
        kernel,
        in_specs=[SM] * len(smem) + [VM] * len(vmem),
        out_specs=[VM] * len(outs),
        out_shape=[pltpu.VMEM(s, F32) for s in outs],
        scratch_shapes=list(scratch),
        compiler_params=LIMIT,
    )
    return run(*smem, *[near(v) for v in vmem])


def swap(value, axis, odd):
    count = lax.axis_size(axis)
    pairs = []
    for i in range(odd, count - 1, 2):
        pairs += [(i, i + 1), (i + 1, i)]
    return lax.ppermute(value, axis, pairs)


def across(value):
    return lax.ppermute(value, "th", [(0, 1), (1, 0)])


SPLIT = [pltpu.VMEM((NX, C, NR, NT), BF16), pltpu.VMEM((NX, C, NR, NT), BF16), pltpu.VMEM((NX, C, NR, NT), F32)]
WIDE_R = pltpu.VMEM((C, NX, 32, NT), F32)


def shards(state, seed, cx, cr, ct, cf, met):
    shapes = [FULL, FULL, RIM, XPAY, XPAY]
    state, seed, prim, xe, xo = pl.pallas_call(
        first,
        in_specs=[pl.BlockSpec(memory_space=pltpu.HBM)] * 3,
        out_specs=[VM] * len(shapes),
        out_shape=[pltpu.VMEM(s, F32) for s in shapes],
        scratch_shapes=[pltpu.SMEM((TAPS,), F32), pltpu.SemaphoreType.DMA((3,))],
        name="first",
        compiler_params=LIMIT,
    )(*[pltpu.with_memory_space_constraint(v, pltpu.HBM) for v in (cf, state, seed)])
    xe = swap(xe, "gx", 0)
    xo = swap(xo, "gx", 1)
    plam, re, ro, th = call(second, [cf, met], [state, seed, prim], [FULL, RPAY, RPAY, TPAY])
    th = across(th)
    re = swap(re, "row", 0)
    ro = swap(ro, "row", 1)
    fx, fr, tt = call(own_flux, [ct], [state], [FULL, (C, NX, 32, NT), (NX, C, NR, NT)], SPLIT[:2])
    (psec,) = call(own, [cx, cr, met], [state, fx, fr, tt], [FULL])
    one = [(C, W, NR, NT)] * 3 + [XPAY2]
    near_args = [seed, psec, plam]
    se, le, lhe, xe2 = call(join_e, [cx, cr, ct, cf, met], near_args + [xe, re, ro, th], one)
    xe2 = swap(xe2, "gx", 0)
    so, lo, lho, xo2 = call(join_o, [cx, cr, ct, cf, met], near_args + [xo, re, ro, th], one)
    xo2 = swap(xo2, "gx", 1)
    full = pltpu.VMEM(FULL, F32)
    inner = pltpu.VMEM((C, NX - 2 * W, NR, NT), F32)
    whole = jax.ShapeDtypeStruct(FULL, F32)
    new, adj, nrim, arim = pl.pallas_call(
        finish,
        in_specs=[SM] * 5 + [VM] * 12,
        out_specs=[ANY, ANY, VM, VM],
        out_shape=[whole, whole, pltpu.VMEM(RIM, F32), pltpu.VMEM(RIM, F32)],
        scratch_shapes=[full, full, pltpu.VMEM((2, C, NR, NT), F32), WIDE_R]
        + SPLIT
        + [inner, inner, pltpu.SemaphoreType.DMA((2,))],
        name="finish",
        compiler_params=LIMIT,
    )(cx, cr, ct, cf, met, *map(near, (state, psec, plam, se, so, le, lo, lhe, lho, re, ro, th)))
    return pl.pallas_call(
        edges,
        in_specs=[SM] * 4 + [VM] * 5 + [ANY] * 2,
        out_specs=[ANY, ANY],
        out_shape=[whole, whole],
        scratch_shapes=[pltpu.VMEM(RIM, F32)] * 2
        + [pltpu.VMEM((C, W, NR, NT), F32)] * 2
        + [pltpu.SemaphoreType.DMA((4,))],
        input_output_aliases={9: 0, 10: 1},
        name="edges",
        compiler_params=LIMIT,
    )(cr, ct, cf, met, *map(near, (state, xe2, xo2, nrim, arim)), new, adj)


def solution(mesh):
    whole = P(None, "gx", "row", "th")

    return jax.shard_map(
        shards,
        mesh=mesh,
        in_specs=(whole, whole, P(), P(), P(), P(), P("row")),
        out_specs=(whole, whole),
        check_vma=False,
    )
```
